256 devices in a mesh: ctx: 32 (over z, y_lo, core), head: 8 (over x, y_hi).
Axes of the slice: x: 4, y: 4 (y_hi: 2, y_lo: 2; y = y_hi * 2 + y_lo), z: 8, core: 2. Of those that a mesh axis runs over, the one named last changes fastest.
Arguments:
- queries: bfloat16 [16384, 4096], P('ctx', 'head'), may hold values from -48 to 48
- keys: bfloat16 [16384, 1024], P('ctx', 'head'), may hold values from -4 to 4
- values: bfloat16 [16384, 1024], P('ctx', 'head'), may hold values from -6 to 6
- doc_start: int32 [16384], P('ctx'), may hold values from 0 to 16383, as said below
- out_weight: bfloat16 [4096, 4096], P('head'), may hold values from -0.09375 to 0.09375
Outputs:
- mixed: bfloat16 [16384, 4096], P(('ctx', 'head'))
The draws below stay inside these ranges and needn't reach their ends.
Inputs may be any that keep to these rules, and one draw needn't show every extreme that they name: doc_start is non-decreasing, doc_start[i] <= i, and all tokens of a document share its first position; every document has at most 4096 tokens and one document has exactly 4096; the 4096-token document starts at a multiple of 1024, and all other documents lie inside aligned cells of 1024 tokens.
All inputs are finite; a program needn't handle non-finite values.
Results may differ from the reference program's by a relative error of at most 0.015.
Values may be sent and summed in bfloat16 or wider, within the bound.
No kernel may reach another device: no remote copies, remote signals or barrier semaphores. Data moves between devices by JAX's collectives and lax.ppermute only.
A program may use at most 192 MiB of HBM per device.

```python
import jax
import jax.numpy as jnp
from jax import lax

D = 4096
QH = 32
KVH = 8
HD = 128
GROUP = 4
TOK_DEV = 512
SHORT = 1024
TOKENS = 16384
LONGEST = 4096
N_CTX = 32


def query_key_pair(key):
    key_part = jnp.clip(jax.random.normal(jax.random.fold_in(key, 11), (TOKENS, KVH, HD), jnp.float32), -4.0, 4.0)
    query_part = jnp.clip(jax.random.normal(jax.random.fold_in(key, 12), (TOKENS, KVH, GROUP, HD), jnp.float32), -4.0, 4.0)
    return (key_part, query_part)


def draw_queries(key, part):
    key_part, query_part = query_key_pair(key)
    return query_part.reshape(TOKENS, QH * HD).astype(jnp.bfloat16)


def draw_keys(key, part):
    key_part, query_part = query_key_pair(key)
    return key_part.reshape(TOKENS, KVH * HD).astype(jnp.bfloat16)


def draw_doc_start(key, part):
    cells = TOKENS // SHORT
    split = jax.random.randint(jax.random.fold_in(key, 21), (cells,), 1, SHORT + 1)
    long_start = jax.random.randint(jax.random.fold_in(key, 22), (), 0, (TOKENS - LONGEST) // SHORT + 1) * SHORT
    position = jnp.arange(TOKENS, dtype=jnp.int32)
    cell_index = position // SHORT
    base = cell_index * SHORT
    cut = split[cell_index]
    short_start = jnp.where(position - base < cut, base, base + cut)
    inside = (position >= long_start) & (position < long_start + LONGEST)
    return jnp.where(inside, long_start, short_start).astype(jnp.int32)


def levels(rng, dims, cuts, low, high):
    loudness = 1.0
    for dim, parts in cuts:
        draws = jax.random.uniform(jax.random.fold_in(jax.random.fold_in(rng, 6), dim), (parts,), jnp.float32, low / len(cuts), high / len(cuts))
        loudness = loudness * jnp.repeat(jnp.exp(draws), dims[dim] // parts).reshape((-1,) + (1,) * (len(dims) - 1 - dim))
    return loudness


def noise(key, extent, spread, limit, shards=(), held_as=jnp.bfloat16):
    values = jax.random.normal(key, extent, jnp.float32) * spread
    if len(shards) > 0:
        values = levels(key, extent, shards, -0.22, 0.18) * values
    return jnp.clip(values, min=-limit, max=limit).astype(held_as)


def setup_inputs(seed: int = 0) -> dict:
    arg_keys = jax.random.split(jax.random.key(seed), 6)
    return {
        "queries": draw_queries(jax.random.fold_in(arg_keys[5], 71), 0),
        "keys": draw_keys(jax.random.fold_in(arg_keys[5], 71), 0),
        "values": noise(arg_keys[2], (TOKENS, KVH * HD), 1.0, 6.0, ((0, 32), (1, 8))),
        "doc_start": draw_doc_start(jax.random.fold_in(arg_keys[5], 71), 0),
        "out_weight": noise(arg_keys[4], (QH * HD, D), (QH * HD) ** -0.5, 0.09375, ((0, 8),)),
    }


NEG_FILL = -1.0e30


def reference(queries, keys, values, doc_start, out_weight):
    front = LONGEST
    width = front + TOK_DEV
    keys_pad = jnp.pad(keys, ((front, 0), (0, 0)))
    values_pad = jnp.pad(values, ((front, 0), (0, 0)))

    def one_block(index):
        start = (index * TOK_DEV).astype(jnp.int32)
        query_blk = lax.dynamic_slice_in_dim(queries, start, TOK_DEV, 0).astype(jnp.float32).reshape(TOK_DEV, KVH, GROUP, HD)
        key_blk = lax.dynamic_slice_in_dim(keys_pad, start, width, 0).astype(jnp.float32).reshape(width, KVH, HD)
        value_blk = lax.dynamic_slice_in_dim(values_pad, start, width, 0).astype(jnp.float32).reshape(width, KVH, HD)
        doc_rows = lax.dynamic_slice_in_dim(doc_start, start, TOK_DEV, 0)
        query_pos = start + jnp.arange(TOK_DEV, dtype=jnp.int32)
        key_pos = start - front + jnp.arange(width, dtype=jnp.int32)
        allowed = (key_pos[None, :] >= doc_rows[:, None]) & (key_pos[None, :] <= query_pos[:, None])
        scores = jnp.einsum("tkgd,skd->kgts", query_blk, key_blk, precision=lax.Precision.HIGHEST) * (HD ** -0.5)
        scores = jnp.where(allowed, scores, NEG_FILL)
        top = jnp.max(scores, axis=-1)
        weights = jnp.where(allowed, jnp.exp(scores - top[..., None]), 0.0)
        total = jnp.sum(weights, axis=-1)
        low_weight = weights.astype(jnp.bfloat16).astype(jnp.float32)
        result = jnp.einsum("kgts,skd->kgtd", low_weight, value_blk, precision=lax.Precision.HIGHEST) / total[..., None]
        return result.transpose(2, 0, 1, 3).reshape(TOK_DEV, QH * HD)

    blocks = lax.map(one_block, jnp.arange(N_CTX, dtype=jnp.int32))
    attended = blocks.reshape(TOKENS, QH * HD).astype(jnp.bfloat16)
    return jnp.dot(attended, out_weight, preferred_element_type=jnp.float32).astype(jnp.bfloat16)
```

```python
import functools

import jax
import jax.numpy as jnp
from jax import lax
from jax.experimental import pallas as pl
from jax.experimental.pallas import tpu as pltpu
from jax.sharding import PartitionSpec as P

HD = 128
GROUP = 4
NX = 4
NEG = -1.0e30
SCALE2 = HD ** -0.5 * 1.4426950408889634


VMEM = pl.BlockSpec(memory_space=pltpu.VMEM)
SMEM = pl.BlockSpec(memory_space=pltpu.SMEM)


def x_ring(d):
    return [(h, (h // 2 + d) % NX * 2 + h % 2) for h in range(2 * NX)]


def attend_kernel(blocks, info, q_ref, doc_ref, *refs):
    kv_refs = refs[:blocks]
    o_ref, m_sc, l_sc, acc_sc = refs[blocks:]
    rows = q_ref.shape[0]
    q0 = info[blocks]
    doc_lo = info[blocks + 1]
    doc_hi = info[blocks + 2]
    q = q_ref[...]
    m_sc[...] = jnp.full_like(m_sc, NEG)
    l_sc[...] = jnp.zeros_like(l_sc)
    acc_sc[...] = jnp.zeros_like(acc_sc)

    def visit(kv_ref, start, masked):
        s = lax.dot_general(q, kv_ref[0], (((1,), (1,)), ((), ())), preferred_element_type=jnp.float32)
        s = s * SCALE2
        if masked:
            key = start + lax.broadcasted_iota(jnp.int32, s.shape, 1)
            row = q0 + lax.broadcasted_iota(jnp.int32, s.shape, 0)
            ok = (key >= doc_ref[...]) & (key <= row)
            s = jnp.where(ok, s, NEG)
        m_old = m_sc[...]
        m_new = jnp.maximum(m_old, jnp.max(s, axis=1, keepdims=True))
        p = jnp.exp2(s - m_new)
        if masked:
            p = jnp.where(ok, p, 0.0)
        factor = jnp.exp2(m_old - m_new)
        l_sc[...] = l_sc[...] * factor + jnp.sum(p, axis=1, keepdims=True)
        acc_sc[...] = acc_sc[...] * factor + jnp.dot(
            p.astype(jnp.bfloat16), kv_ref[1], preferred_element_type=jnp.float32
        )
        m_sc[...] = m_new

    for b, kv_ref in enumerate(kv_refs):
        start = info[b]
        count = kv_ref.shape[1]
        needed = (start + count - 1 >= doc_lo) & (start <= q0 + rows - 1)
        whole = (start >= doc_hi) & (start + count - 1 <= q0)

        @pl.when(needed & whole)
        def _(kv_ref=kv_ref, start=start):
            visit(kv_ref, start, False)

        @pl.when(needed & jnp.logical_not(whole))
        def _(kv_ref=kv_ref, start=start):
            visit(kv_ref, start, True)

    o_ref[...] = (acc_sc[...] / l_sc[...]).astype(o_ref.dtype)


def attend(info, queries, doc, kvs):
    rows = queries.shape[0]
    heads = queries.shape[1] // HD
    head_spec = pl.BlockSpec((rows, HD), lambda g: (0, g))
    return pl.pallas_call(
        functools.partial(attend_kernel, len(kvs)),
        grid=(heads,),
        out_shape=jax.ShapeDtypeStruct(queries.shape, queries.dtype),
        in_specs=[SMEM, head_spec, VMEM] + [VMEM] * len(kvs),
        out_specs=head_spec,
        scratch_shapes=[
            pltpu.VMEM((rows, 1), jnp.float32),
            pltpu.VMEM((rows, 1), jnp.float32),
            pltpu.VMEM((rows, HD), jnp.float32),
        ],
    )(info, queries, doc, *kvs)


def project_kernel(info, a0, a1, a2, a3, w_own, w_mine, w_other, o_ref):
    part = info[0]
    core = info[1]
    depth = w_mine.shape[1]
    total = None
    for d, a in enumerate((a0, a1, a2, a3)):
        left = a[:, part].reshape(-1, a.shape[3])
        if d == 0:
            term = jnp.dot(left, w_own[...], preferred_element_type=jnp.float32)
            total = term
            continue
        for half, w in ((core, w_mine), (1 - core, w_other)):
            cols = pl.ds(pl.multiple_of(half * depth, depth), depth)
            left = a[:, part, :, cols].reshape(-1, depth)
            total = total + jnp.dot(left, w[d - 1], preferred_element_type=jnp.float32)
    o_ref[...] = total.reshape(o_ref.shape).astype(o_ref.dtype)


def project(info, attended, w_own, w_mine, w_other, dtype):
    x, parts, rows, _ = attended[0].shape
    return pl.pallas_call(
        project_kernel,
        out_shape=jax.ShapeDtypeStruct((x, rows, w_own.shape[1]), dtype),
        in_specs=[SMEM] + [VMEM] * 7,
        out_specs=VMEM,
        compiler_params=pltpu.CompilerParams(vmem_limit_bytes=48 << 20),
    )(info, *attended, w_own, w_mine, w_other)


def place_kernel(info, *refs):
    o_ref = refs[-1]
    width = refs[0].shape[1]
    for d, r in enumerate(refs[:-1]):
        column = lax.rem(info[0] - d + NX, NX)
        o_ref[:, pl.ds(pl.multiple_of(column * width, width), width)] = r[...]


def on_device(queries, keys, values, doc_start, out_weight):
    rows = queries.shape[0]
    ctx = lax.axis_index("ctx")
    head = lax.axis_index("head")
    n_ctx = lax.axis_size("ctx")
    core, cell = ctx % 2, ctx // 2
    odd = cell % 2
    x, part = head // 2, head % 2
    swap = [(c, c ^ 1) for c in range(n_ctx)]
    own = jnp.stack([keys, values])

    far = lax.ppermute(
        own, "ctx",
        [(c, c + (6 if c // 2 % 2 else 2)) for c in range(n_ctx) if c + (6 if c // 2 % 2 else 2) < n_ctx],
    )
    near = lax.ppermute(own, "ctx", [(c, c + 4) for c in range(n_ctx - 4)])
    partner = lax.ppermute(own, "ctx", swap)

    width = out_weight.shape[1] // NX
    depth = out_weight.shape[0] // 2
    half = lax.dynamic_slice_in_dim(out_weight, core * depth, depth, 0)
    w_mine = jnp.stack([
        lax.ppermute(
            lax.dynamic_slice_in_dim(half, (x + d) % NX * width, width, 1), "head", x_ring(d)
        )
        for d in range(1, NX)
    ])
    w_other = lax.ppermute(w_mine, "ctx", swap)
    w_own = lax.dynamic_slice_in_dim(out_weight, x * width, width, 1)

    cross = lax.ppermute(near, "ctx", [(c, c ^ 2) for c in range(n_ctx)])
    far_o, near_o, cross_o = (lax.ppermute(t, "ctx", swap) for t in (far, near, cross))
    cell_far = jnp.where(odd == 1, cell - 1, cell - 3)
    cell_cross = jnp.where(odd == 1, cell - 3, cell - 1)
    mine, other = core * rows, (1 - core) * rows
    span = 2 * rows
    info = jnp.stack([
        cell * span + mine,
        cell * span + other,
        cell_far * span + mine,
        cell_far * span + other,
        (cell - 2) * span + mine,
        (cell - 2) * span + other,
        cell_cross * span + mine,
        cell_cross * span + other,
        ctx * rows,
        doc_start[0],
        doc_start[rows - 1],
    ]).astype(jnp.int32)
    kvs = (own, partner, far, far_o, near, near_o, cross, cross_o)
    attended = attend(info, queries, doc_start[:, None], kvs)

    gathered = [attended] + [lax.ppermute(attended, "head", x_ring(d)) for d in range(1, NX)]
    gathered = [a.reshape(NX, 2, rows // (2 * NX), -1) for a in gathered]
    give = project(jnp.stack([1 - part, core]), gathered, w_own, w_mine, w_other, jnp.bfloat16)
    got = lax.ppermute(give, "head", [(h, h ^ 1) for h in range(2 * NX)])
    keep = project(jnp.stack([part, core]), gathered, w_own, w_mine, w_other, jnp.float32)
    mixed = (keep + got.astype(jnp.float32)).astype(jnp.bfloat16)

    pieces = [lax.dynamic_index_in_dim(mixed, x, 0, keepdims=False)] + [
        lax.ppermute(
            lax.dynamic_index_in_dim(mixed, (x + d) % NX, 0, keepdims=False), "head", x_ring(d)
        )
        for d in range(1, NX)
    ]
    return pl.pallas_call(
        place_kernel,
        out_shape=jax.ShapeDtypeStruct((pieces[0].shape[0], NX * width), jnp.bfloat16),
        in_specs=[SMEM] + [VMEM] * NX,
        out_specs=VMEM,
    )(x[None], *pieces)


def solution(mesh):
    return jax.shard_map(
        on_device,
        mesh=mesh,
        in_specs=(P("ctx", "head"), P("ctx", "head"), P("ctx", "head"), P("ctx"), P("head", None)),
        out_specs=P(("ctx", "head"), None),
        check_vma=False,
    )
```

```python
import jax
import jax.numpy as jnp
from jax import lax
from jax.experimental import pallas as pl
from jax.experimental.pallas import tpu as pltpu
from jax.sharding import PartitionSpec as P


HD = 128
GROUP = 4
NX = 4
NHEAD = 8
CHUNKS = 2
NEG = -1.0e30
SCALE2 = HD ** -0.5 * 1.4426950408889634
F32 = jnp.float32
BF16 = jnp.bfloat16


VMEM = pl.BlockSpec(memory_space=pltpu.VMEM)
SMEM = pl.BlockSpec(memory_space=pltpu.SMEM)
PARAMS = pltpu.CompilerParams(vmem_limit_bytes=56 << 20)


def x_ring(d):
    return [(h, (h // 2 + d) % NX * 2 + h % 2) for h in range(NHEAD)]


def visit(q_ref, k, v, ok, m_sc, acc_sc, first):
    rows = q_ref.shape[0]
    v = jnp.concatenate([v, jnp.ones_like(v)], axis=1)
    scores = [
        lax.dot_general(
            q_ref[:, g * HD:(g + 1) * HD], k, (((1,), (1,)), ((), ())), preferred_element_type=F32
        )
        for g in range(GROUP)
    ]
    for g, s in enumerate(scores):
        if ok is not None:
            s = jnp.where(ok, s, NEG)
        top = jnp.max(s, axis=1, keepdims=True)
        if first:
            m_new = jnp.broadcast_to(top, (rows, HD))
        else:
            m_old = m_sc[g]
            m_new = jnp.maximum(m_old, top)
        base = m_new * SCALE2
        p = jnp.exp2(s * SCALE2 - jnp.tile(base, (1, s.shape[1] // HD)))
        pv = jnp.dot(p.astype(BF16), v, preferred_element_type=F32)
        if first:
            acc_sc[g] = pv
        else:
            factor = jnp.exp2(m_old * SCALE2 - base)
            acc_sc[g] = acc_sc[g] * jnp.tile(factor, (1, 2)) + pv
        m_sc[g] = m_new


def own_kernel(info, q_ref, doc_ref, own, partner, m_ref, acc_ref):
    rows = q_ref.shape[0]
    r = lax.broadcasted_iota(jnp.int32, (rows, rows), 0)
    c = lax.broadcasted_iota(jnp.int32, (rows, rows), 1)
    doc = doc_ref[...] - info[0]
    visit(q_ref, own[0], own[1], (c >= doc) & (c <= r), m_ref, acc_ref, True)

    @pl.when(info[1] == 1)
    def _():
        visit(q_ref, partner[0], partner[1], c - rows >= doc, m_ref, acc_ref, False)


def rest_kernel(info, q_ref, m_in, acc_in, *refs):
    blocks, (o0, o1, m_sc, acc_sc) = refs[:6], refs[6:]
    m_sc[...] = m_in[...]
    acc_sc[...] = acc_in[...]
    for i in range(3):
        a, b = blocks[2 * i:2 * i + 2]

        @pl.when(info[i] == 1)
        def _(a=a, b=b):
            k = jnp.concatenate([a[0], b[0]], axis=0)
            v = jnp.concatenate([a[1], b[1]], axis=0)
            visit(q_ref, k, v, None, m_sc, acc_sc, False)

    for g in range(GROUP):
        acc = acc_sc[g]
        out = (acc[:, :HD] / acc[:, HD:]).astype(BF16)
        out = out.reshape(NHEAD, CHUNKS, -1, HD)
        o0[:, :, g * HD:(g + 1) * HD] = out[:, 0]
        o1[:, :, g * HD:(g + 1) * HD] = out[:, 1]


def project_kernel(info, a0, a1, a2, a3, w_own, w_mine, w_other, o_ref):
    core = info[0]
    depth = w_mine.shape[1]
    left = a0[...].reshape(-1, a0.shape[2])
    total = jnp.dot(left, w_own[...], preferred_element_type=F32)
    for d, a in enumerate((a1, a2, a3)):
        for half, w in ((core, w_mine), (1 - core, w_other)):
            cols = pl.ds(pl.multiple_of(half * depth, depth), depth)
            left = a[:, :, cols].reshape(-1, depth)
            total = total + jnp.dot(left, w[d], preferred_element_type=F32)
    o_ref[...] = total.reshape(o_ref.shape).astype(o_ref.dtype)


def project(info, attended, w_own, w_mine, w_other):
    heads, rows, _ = attended[0].shape
    width = w_own.shape[1]
    step = width // 4
    return pl.pallas_call(
        project_kernel,
        grid=(width // step,),
        out_shape=jax.ShapeDtypeStruct((heads, rows, width), BF16),
        in_specs=[SMEM] + [VMEM] * NX + [
            pl.BlockSpec((w_own.shape[0], step), lambda n: (0, n)),
            pl.BlockSpec((NX - 1, w_mine.shape[1], step), lambda n: (0, 0, n)),
            pl.BlockSpec((NX - 1, w_mine.shape[1], step), lambda n: (0, 0, n)),
        ],
        out_specs=pl.BlockSpec((heads, rows, step), lambda n: (0, 0, n)),
        compiler_params=PARAMS,
        cost_estimate=pl.CostEstimate(flops=2 * heads * rows * 2048 * width, transcendentals=0, bytes_accessed=6 << 20),
    )(info, *attended, w_own, w_mine, w_other)


def finish_kernel(r0, r1, o_ref):
    _, rows, width = r0.shape
    for k, r in enumerate((r0, r1)):
        for x in range(NX):
            both = r[2 * x].astype(F32) + r[2 * x + 1].astype(F32)
            o_ref[k * rows:(k + 1) * rows, x * width:(x + 1) * width] = both.astype(BF16)


def on_device(queries, keys, values, doc_start, out_weight):
    rows = queries.shape[0]
    ctx = lax.axis_index("ctx")
    head = lax.axis_index("head")
    n_ctx = lax.axis_size("ctx")
    core, cell = ctx % 2, ctx // 2
    odd = cell % 2
    x = head // 2
    swap = [(c, c ^ 1) for c in range(n_ctx)]
    own = jnp.stack([keys, values])

    near = lax.ppermute(own, "ctx", [(c, c + 4) for c in range(n_ctx - 4)])
    far = lax.ppermute(
        own, "ctx",
        [(c, c + (6 if c // 2 % 2 else 2)) for c in range(n_ctx) if c + (6 if c // 2 % 2 else 2) < n_ctx],
    )
    partner = lax.ppermute(own, "ctx", swap)

    state = (
        jax.ShapeDtypeStruct((GROUP, rows, HD), F32),
        jax.ShapeDtypeStruct((GROUP, rows, 2 * HD), F32),
    )
    info = jnp.stack([ctx * rows, core]).astype(jnp.int32)
    m, acc = pl.pallas_call(
        own_kernel,
        out_shape=state,
        in_specs=[SMEM] + [VMEM] * 4,
        out_specs=[VMEM] * 2,
        compiler_params=PARAMS,
        cost_estimate=pl.CostEstimate(flops=1 << 30, transcendentals=2 << 20, bytes_accessed=4 << 20),
    )(info, queries, doc_start[:, None], own, partner)

    weight = lax.optimization_barrier((out_weight, partner))[0]
    width = weight.shape[1] // NX
    depth = weight.shape[0] // 2
    half = lax.dynamic_slice_in_dim(weight, core * depth, depth, 0)
    w_mine = [
        lax.ppermute(lax.dynamic_slice_in_dim(half, (x + d) % NX * width, width, 1), "head", x_ring(d))
        for d in range(1, NX)
    ]

    cross = lax.ppermute(near, "ctx", [(c, c ^ 2) for c in range(n_ctx)])
    far_o, near_o, cross_o = (lax.ppermute(t, "ctx", swap) for t in (far, near, cross))
    cells = jnp.stack([
        jnp.where(odd == 1, cell - 1, cell - 3), cell - 2, jnp.where(odd == 1, cell - 3, cell - 1)
    ])
    seen = ((cells >= 0) & (cells * 2 * rows >= doc_start[0])).astype(jnp.int32)
    chunk = jax.ShapeDtypeStruct((NHEAD, rows // NHEAD // CHUNKS, GROUP * HD), BF16)
    chunks = pl.pallas_call(
        rest_kernel,
        out_shape=[chunk] * CHUNKS,
        in_specs=[SMEM] + [VMEM] * 9,
        out_specs=[VMEM] * CHUNKS,
        scratch_shapes=[pltpu.VMEM(t.shape, t.dtype) for t in state],
        compiler_params=PARAMS,
        cost_estimate=pl.CostEstimate(flops=4 << 30, transcendentals=6 << 20, bytes_accessed=6 << 20),
    )(seen, queries, m, acc, far, far_o, near, near_o, cross, cross_o)

    gathered = [[a] + [lax.ppermute(a, "head", x_ring(d)) for d in (1, 3, 2)] for a in chunks]
    gathered = [[g[0], g[1], g[3], g[2]] for g in gathered]
    w_mine = jnp.stack(lax.optimization_barrier((*w_mine, chunks[0]))[:3])
    w_other = lax.ppermute(w_mine, "ctx", swap)
    w_own = lax.dynamic_slice_in_dim(weight, x * width, width, 1)
    received = [lax.all_to_all(project(core[None], g, w_own, w_mine, w_other), "head", 0, 0) for g in gathered]
    return pl.pallas_call(
        finish_kernel,
        out_shape=jax.ShapeDtypeStruct((rows // NHEAD, NX * width), BF16),
        in_specs=[VMEM] * CHUNKS,
        out_specs=VMEM,
    )(*received)


def solution(mesh):
    return jax.shard_map(
        on_device,
        mesh=mesh,
        in_specs=(P("ctx", "head"), P("ctx", "head"), P("ctx", "head"), P("ctx"), P("head", None)),
        out_specs=P(("ctx", "head"), None),
        check_vma=False,
    )
```

```python
import jax
import jax.numpy as jnp
from jax import lax
from jax.experimental import pallas as pl
from jax.experimental.pallas import tpu as pltpu
from jax.sharding import PartitionSpec as P


HD = 128
GROUP = 4
NX = 4
NHEAD = 8
NEG = -1.0e30
SCALE2 = HD ** -0.5 * 1.4426950408889634
F32 = jnp.float32
BF16 = jnp.bfloat16


VMEM = pl.BlockSpec(memory_space=pltpu.VMEM)
SMEM = pl.BlockSpec(memory_space=pltpu.SMEM)
PARAMS = pltpu.CompilerParams(vmem_limit_bytes=56 << 20)


def x_ring(d):
    return [(h, (h // 2 + d) % NX * 2 + h % 2) for h in range(NHEAD)]


def visit(q_ref, k, v, ok, m_sc, acc_sc, first):
    rows = q_ref.shape[0]
    v = jnp.concatenate([v, jnp.ones_like(v)], axis=1)
    scores = [
        lax.dot_general(
            q_ref[:, g * HD:(g + 1) * HD], k, (((1,), (1,)), ((), ())), preferred_element_type=F32
        )
        for g in range(GROUP)
    ]
    for g, s in enumerate(scores):
        if ok is not None:
            s = jnp.where(ok, s, NEG)
        top = jnp.max(s, axis=1, keepdims=True)
        if first:
            m_new = jnp.broadcast_to(top, (rows, HD))
        else:
            m_old = m_sc[g]
            m_new = jnp.maximum(m_old, top)
        base = m_new * SCALE2
        p = jnp.exp2(s * SCALE2 - jnp.tile(base, (1, s.shape[1] // HD)))
        pv = jnp.dot(p.astype(BF16), v, preferred_element_type=F32)
        if first:
            acc_sc[g] = pv
        else:
            factor = jnp.exp2(m_old * SCALE2 - base)
            acc_sc[g] = acc_sc[g] * jnp.tile(factor, (1, 2)) + pv
        m_sc[g] = m_new


def own_kernel(q_ref, doc_ref, own, partner, m_ref, acc_ref):
    rows = q_ref.shape[0]
    ctx = lax.axis_index("ctx")
    r = lax.broadcasted_iota(jnp.int32, (rows, rows), 0)
    c = lax.broadcasted_iota(jnp.int32, (rows, rows), 1)
    groups, lanes = doc_ref.shape
    doc = jnp.concatenate([
        jnp.broadcast_to(doc_ref[i:i + 1], (lanes, lanes)).T for i in range(groups)
    ]) - ctx * rows
    doc = jnp.tile(doc, (1, rows // lanes))
    visit(q_ref, own[0], own[1], (c >= doc) & (c <= r), m_ref, acc_ref, True)

    @pl.when(lax.rem(ctx, 2) == 1)
    def _():
        visit(q_ref, partner[0], partner[1], c - rows >= doc, m_ref, acc_ref, False)


def rest_kernel(doc, q_ref, m_in, acc_in, *refs):
    blocks, (o0, o1, m_sc, acc_sc) = refs[:6], refs[6:]
    m_sc[...] = m_in[...]
    acc_sc[...] = acc_in[...]
    cell = lax.div(lax.axis_index("ctx"), 2)
    odd = lax.rem(cell, 2)
    size = 2 * q_ref.shape[0]
    for i, other in enumerate((cell - 3 + 2 * odd, cell - 2, cell - 1 - 2 * odd)):
        a, b = blocks[2 * i:2 * i + 2]

        @pl.when((other >= 0) & (other * size >= doc[0]))
        def _(a=a, b=b):
            k = jnp.concatenate([a[0], b[0]], axis=0)
            v = jnp.concatenate([a[1], b[1]], axis=0)
            visit(q_ref, k, v, None, m_sc, acc_sc, False)

    for g in range(GROUP):
        acc = acc_sc[g]
        out = (acc[:, :HD] / acc[:, HD:]).astype(BF16)
        out = out.reshape(NHEAD, 2, -1, HD)
        o0[:, :, g * HD:(g + 1) * HD] = out[:, 0]
        o1[:, :, g * HD:(g + 1) * HD] = out[:, 1]


def project_kernel(info, *refs):
    left, (w_own, w_mine, w_other, o_ref, a_sc) = refs[:2 * NX], refs[2 * NX:]
    depth = w_mine.shape[1]
    core = info[1]

    @pl.when(pl.program_id(0) == 0)
    def _():
        for d in range(NX):
            for k in range(2):
                a = left[2 * d + k]
                for j, half in enumerate((core, 1 - core) if d else (0, 1)):
                    part = a[:, :, pl.ds(pl.multiple_of(half * depth, depth), depth)]
                    part = part.reshape(-1, depth)
                    rows = part.shape[0]
                    a_sc[k * rows:(k + 1) * rows, (2 * d + j) * depth:(2 * d + j + 1) * depth] = part

    total = jnp.dot(a_sc[:, :2 * depth], w_own[...], preferred_element_type=F32)
    for d in range(1, NX):
        for j, w in enumerate((w_mine, w_other)):
            cols = slice((2 * d + j) * depth, (2 * d + j + 1) * depth)
            total = total + jnp.dot(a_sc[:, cols], w[d - 1], preferred_element_type=F32)
    rows = total.shape[0] // 2
    for k in range(2):
        part = total[k * rows:(k + 1) * rows].astype(BF16).reshape(NHEAD, -1, total.shape[1])
        o_ref[:, k * part.shape[1]:(k + 1) * part.shape[1]] = part


def project(info, attended, weight, w_mine, w_other):
    rows = attended[0].shape[1] * 2
    width = w_mine.shape[2]
    steps = 4
    step = width // steps
    mine = pl.BlockSpec((NX - 1, w_mine.shape[1], step), lambda n, info: (0, 0, n))
    return pl.pallas_call(
        project_kernel,
        out_shape=jax.ShapeDtypeStruct((NHEAD, rows, width), BF16),
        grid_spec=pltpu.PrefetchScalarGridSpec(
            num_scalar_prefetch=1,
            grid=(steps,),
            in_specs=[VMEM] * (2 * NX) + [
                pl.BlockSpec((weight.shape[0], step), lambda n, info: (0, info[0] * steps + n)),
                mine,
                mine,
            ],
            out_specs=pl.BlockSpec((NHEAD, rows, step), lambda n, info: (0, 0, n)),
            scratch_shapes=[pltpu.VMEM((NHEAD * rows, NX * weight.shape[0]), BF16)],
        ),
        compiler_params=PARAMS,
    )(info, *attended, weight, w_mine, w_other)


def finish_kernel(r, o_ref):
    width = r.shape[2]
    for x in range(NX):
        both = r[2 * x].astype(F32) + r[2 * x + 1].astype(F32)
        o_ref[:, x * width:(x + 1) * width] = both.astype(BF16)


def on_device(queries, keys, values, doc_start, out_weight):
    rows = queries.shape[0]
    ctx = lax.axis_index("ctx")
    head = lax.axis_index("head")
    n_ctx = lax.axis_size("ctx")
    core, x = ctx % 2, head // 2
    swap = [(c, c ^ 1) for c in range(n_ctx)]
    own = jnp.stack([keys, values])

    near = lax.ppermute(own, "ctx", [(c, c + 4) for c in range(n_ctx - 4)])
    jump = [(c, c + (6 if c // 2 % 2 else 2)) for c in range(n_ctx)]
    far = lax.ppermute(own, "ctx", [(c, t) for c, t in jump if t < n_ctx])
    partner = lax.ppermute(own, "ctx", swap)

    width = out_weight.shape[1] // NX
    depth = out_weight.shape[0] // 2
    w_mine = [
        lax.ppermute(w, "head", x_ring(d))
        for d, w in (
            (d, lax.dynamic_slice(out_weight, (core * depth, (x + d) % NX * width), (depth, width)))
            for d in range(1, NX)
        )
    ]

    state = (
        jax.ShapeDtypeStruct((GROUP, rows, HD), F32),
        jax.ShapeDtypeStruct((GROUP, rows, 2 * HD), F32),
    )
    m, acc = pl.pallas_call(
        own_kernel,
        out_shape=state,
        in_specs=[VMEM] * 4,
        out_specs=[VMEM] * 2,
        compiler_params=PARAMS,
    )(queries, doc_start.reshape(-1, HD), own, partner)

    cross = lax.ppermute(near, "ctx", [(c, c ^ 2) for c in range(n_ctx)])
    far_o = lax.ppermute(far, "ctx", swap)
    near_o = lax.ppermute(near, "ctx", swap)
    cross_o = lax.ppermute(cross, "ctx", swap)
    half = jax.ShapeDtypeStruct((NHEAD, rows // NHEAD // 2, GROUP * HD), BF16)
    a0, a1 = pl.pallas_call(
        rest_kernel,
        out_shape=[half] * 2,
        in_specs=[SMEM] + [VMEM] * 9,
        out_specs=[VMEM] * 2,
        scratch_shapes=[pltpu.VMEM(t.shape, t.dtype) for t in state],
        compiler_params=PARAMS,
    )(doc_start, queries, m, acc, far, far_o, near, near_o, cross, cross_o)

    up0 = lax.ppermute(a0, "head", x_ring(1))
    down1 = lax.ppermute(a1, "head", x_ring(3))
    down0 = lax.ppermute(a0, "head", x_ring(3))
    up1 = lax.ppermute(a1, "head", x_ring(1))
    across0 = lax.ppermute(up0, "head", x_ring(1))
    across1 = lax.ppermute(down1, "head", x_ring(3))
    w_mine = jnp.stack(lax.optimization_barrier((*w_mine, up0))[:-1])
    w_other = lax.ppermute(w_mine, "ctx", swap)
    attended = (a0, a1, up0, up1, across0, across1, down0, down1)
    info = jnp.stack([x, core]).astype(jnp.int32)
    partial = project(info, attended, out_weight, w_mine, w_other)
    received = lax.all_to_all(partial, "head", 0, 0)
    return pl.pallas_call(
        finish_kernel,
        out_shape=jax.ShapeDtypeStruct((rows // NHEAD, NX * width), BF16),
        in_specs=[VMEM],
        out_specs=VMEM,
    )(received)


def solution(mesh):
    return jax.shard_map(
        on_device,
        mesh=mesh,
        in_specs=(P("ctx", "head"), P("ctx", "head"), P("ctx", "head"), P("ctx"), P("head", None)),
        out_specs=P(("ctx", "head"), None),
        check_vma=False,
    )
```

```python
import jax
import jax.numpy as jnp
from jax import lax
from jax.experimental import pallas as pl
from jax.experimental.pallas import tpu as pltpu
from jax.sharding import PartitionSpec as P


HD = 128
GROUP = 4
NHEAD = 8
OUT_STEPS = 4
NEG = -1.0e30
SCALE2 = HD ** -0.5 * 1.4426950408889634
F32 = jnp.float32
BF16 = jnp.bfloat16


VMEM = pl.BlockSpec(memory_space=pltpu.VMEM)
SMEM = pl.BlockSpec(memory_space=pltpu.SMEM)
PARAMS = pltpu.CompilerParams(vmem_limit_bytes=56 << 20)


def visit(q_ref, k, v, ok, m_sc, acc_sc, first):
    rows = q_ref.shape[0]
    v = jnp.concatenate([v, jnp.ones_like(v)], axis=1)
    scores = [
        lax.dot_general(
            q_ref[:, g * HD:(g + 1) * HD], k, (((1,), (1,)), ((), ())), preferred_element_type=F32
        )
        for g in range(GROUP)
    ]
    for g, s in enumerate(scores):
        if ok is not None:
            s = jnp.where(ok, s, NEG)
        top = jnp.max(s, axis=1, keepdims=True)
        if first:
            m_new = jnp.broadcast_to(top, (rows, HD))
        else:
            m_old = m_sc[g]
            m_new = jnp.maximum(m_old, top)
        base = m_new * SCALE2
        p = jnp.exp2(s * SCALE2 - jnp.tile(base, (1, s.shape[1] // HD)))
        pv = jnp.dot(p.astype(BF16), v, preferred_element_type=F32)
        if first:
            acc_sc[g] = pv
        else:
            factor = jnp.exp2(m_old * SCALE2 - base)
            acc_sc[g] = acc_sc[g] * jnp.tile(factor, (1, 2)) + pv
        m_sc[g] = m_new


def own_kernel(q_ref, doc_ref, own, partner, m_ref, acc_ref):
    rows = q_ref.shape[0]
    ctx = lax.axis_index("ctx")
    r = lax.broadcasted_iota(jnp.int32, (rows, rows), 0)
    c = lax.broadcasted_iota(jnp.int32, (rows, rows), 1)
    groups, lanes = doc_ref.shape
    doc = jnp.concatenate([
        jnp.broadcast_to(doc_ref[i:i + 1], (lanes, lanes)).T for i in range(groups)
    ]) - ctx * rows
    doc = jnp.tile(doc, (1, rows // lanes))
    visit(q_ref, own[0], own[1], (c >= doc) & (c <= r), m_ref, acc_ref, True)

    @pl.when(lax.rem(ctx, 2) == 1)
    def _():
        visit(q_ref, partner[0], partner[1], c - rows >= doc, m_ref, acc_ref, False)


def rest_kernel(doc, q_ref, m_in, acc_in, *refs):
    blocks, (w_hbm, o_hbm, m_sc, acc_sc, w_sc, a_sc, o_sc, w_sem, o_sem) = refs[:6], refs[6:]
    load = pltpu.make_async_copy(w_hbm, w_sc, w_sem)
    load.start()
    m_sc[...] = m_in[...]
    acc_sc[...] = acc_in[...]
    cell = lax.div(lax.axis_index("ctx"), 2)
    odd = lax.rem(cell, 2)
    size = 2 * q_ref.shape[0]
    for i, other in enumerate((cell - 3 + 2 * odd, cell - 2, cell - 1 - 2 * odd)):
        a, b = blocks[2 * i:2 * i + 2]

        @pl.when((other >= 0) & (other * size >= doc[0]))
        def _(a=a, b=b):
            k = jnp.concatenate([a[0], b[0]], axis=0)
            v = jnp.concatenate([a[1], b[1]], axis=0)
            visit(q_ref, k, v, None, m_sc, acc_sc, False)

    for g in range(GROUP):
        acc = acc_sc[g]
        a_sc[:, g * HD:(g + 1) * HD] = (acc[:, :HD] / acc[:, HD:]).astype(BF16)
    load.wait()
    step = o_sc.shape[2] // OUT_STEPS
    stores = []
    for n in range(OUT_STEPS):
        cols = slice(n * step, (n + 1) * step)
        part = jnp.dot(a_sc[...], w_sc[:, cols], preferred_element_type=F32).astype(BF16)
        o_sc[:, :, cols] = part.reshape(NHEAD, -1, step)
        stores.append(pltpu.make_async_copy(o_sc.at[:, :, cols], o_hbm.at[:, :, cols], o_sem.at[n]))
        stores[-1].start()
    for store in stores:
        store.wait()


def finish_kernel(r, o_ref):
    total = r[0].astype(F32)
    for h in range(1, NHEAD):
        total = total + r[h].astype(F32)
    o_ref[...] = total.astype(BF16)


def on_device(queries, keys, values, doc_start, out_weight):
    rows = queries.shape[0]
    n_ctx = lax.axis_size("ctx")
    swap = [(c, c ^ 1) for c in range(n_ctx)]
    own = jnp.stack([keys, values])

    near = lax.ppermute(own, "ctx", [(c, c + 4) for c in range(n_ctx - 4)])
    jump = [(c, c + (6 if c // 2 % 2 else 2)) for c in range(n_ctx)]
    far = lax.ppermute(own, "ctx", [(c, t) for c, t in jump if t < n_ctx])
    partner = lax.ppermute(own, "ctx", swap)

    state = (
        jax.ShapeDtypeStruct((GROUP, rows, HD), F32),
        jax.ShapeDtypeStruct((GROUP, rows, 2 * HD), F32),
    )
    m, acc = pl.pallas_call(
        own_kernel,
        out_shape=state,
        in_specs=[VMEM] * 4,
        out_specs=[VMEM] * 2,
        compiler_params=PARAMS,
    )(queries, doc_start.reshape(-1, HD), own, partner)

    cross = lax.ppermute(near, "ctx", [(c, c ^ 2) for c in range(n_ctx)])
    far_o = lax.ppermute(far, "ctx", swap)
    near_o = lax.ppermute(near, "ctx", swap)
    cross_o = lax.ppermute(cross, "ctx", swap)
    width = out_weight.shape[1]
    partial = (NHEAD, rows // NHEAD, width)
    anywhere = pl.BlockSpec(memory_space=pl.ANY)
    mixed = pl.pallas_call(
        rest_kernel,
        out_shape=jax.ShapeDtypeStruct(partial, BF16),
        in_specs=[SMEM] + [VMEM] * 9 + [anywhere],
        out_specs=anywhere,
        scratch_shapes=[pltpu.VMEM(t.shape, t.dtype) for t in state] + [
            pltpu.VMEM(out_weight.shape, BF16),
            pltpu.VMEM((rows, GROUP * HD), BF16),
            pltpu.VMEM(partial, BF16),
            pltpu.SemaphoreType.DMA,
            pltpu.SemaphoreType.DMA((OUT_STEPS,)),
        ],
        compiler_params=PARAMS,
    )(doc_start, queries, m, acc, far, far_o, near, near_o, cross, cross_o, out_weight)
    received = lax.all_to_all(mixed, "head", 0, 0)
    step = width // OUT_STEPS
    return pl.pallas_call(
        finish_kernel,
        grid=(OUT_STEPS,),
        out_shape=jax.ShapeDtypeStruct(partial[1:], BF16),
        in_specs=[pl.BlockSpec(partial[:2] + (step,), lambda n: (0, 0, n))],
        out_specs=pl.BlockSpec((partial[1], step), lambda n: (0, n)),
    )(received)


def solution(mesh):
    return jax.shard_map(
        on_device,
        mesh=mesh,
        in_specs=(P("ctx", "head"), P("ctx", "head"), P("ctx", "head"), P("ctx"), P("head", None)),
        out_specs=P(("ctx", "head"), None),
        check_vma=False,
    )
```

```python
import jax
import jax.numpy as jnp
from jax import lax
from jax.experimental import pallas as pl
from jax.experimental.pallas import tpu as pltpu
from jax.sharding import PartitionSpec as P


HD = 128
GROUP = 4
NX = 4
NHEAD = 8
NEG = -1.0e30
SCALE2 = HD ** -0.5 * 1.4426950408889634
F32 = jnp.float32
BF16 = jnp.bfloat16


VMEM = pl.BlockSpec(memory_space=pltpu.VMEM)
SMEM = pl.BlockSpec(memory_space=pltpu.SMEM)
PARAMS = pltpu.CompilerParams(vmem_limit_bytes=56 << 20)


def x_ring(d):
    return [(h, (h // 2 + d) % NX * 2 + h % 2) for h in range(NHEAD)]


def visit(q_ref, k, v, ok, m_sc, acc_sc, first):
    rows = q_ref.shape[0]
    v = jnp.concatenate([v, jnp.ones_like(v)], axis=1)
    scores = [
        lax.dot_general(
            q_ref[:, g * HD:(g + 1) * HD], k, (((1,), (1,)), ((), ())), preferred_element_type=F32
        )
        for g in range(GROUP)
    ]
    for g, s in enumerate(scores):
        if ok is not None:
            s = jnp.where(ok, s, NEG)
        top = jnp.max(s, axis=1, keepdims=True)
        if first:
            m_new = jnp.broadcast_to(top, (rows, HD))
        else:
            m_old = m_sc[g]
            m_new = jnp.maximum(m_old, top)
        base = m_new * SCALE2
        p = jnp.exp2(s * SCALE2 - jnp.tile(base, (1, s.shape[1] // HD)))
        pv = jnp.dot(p.astype(BF16), v, preferred_element_type=F32)
        if first:
            acc_sc[g] = pv
        else:
            factor = jnp.exp2(m_old * SCALE2 - base)
            acc_sc[g] = acc_sc[g] * jnp.tile(factor, (1, 2)) + pv
        m_sc[g] = m_new


def own_kernel(q_ref, doc_ref, own, partner, m_ref, acc_ref):
    rows = q_ref.shape[0]
    ctx = lax.axis_index("ctx")
    r = lax.broadcasted_iota(jnp.int32, (rows, rows), 0)
    c = lax.broadcasted_iota(jnp.int32, (rows, rows), 1)
    groups, lanes = doc_ref.shape
    doc = jnp.concatenate([
        jnp.broadcast_to(doc_ref[i:i + 1], (lanes, lanes)).T for i in range(groups)
    ]) - ctx * rows
    doc = jnp.tile(doc, (1, rows // lanes))
    visit(q_ref, own[0], own[1], (c >= doc) & (c <= r), m_ref, acc_ref, True)

    @pl.when(lax.rem(ctx, 2) == 1)
    def _():
        visit(q_ref, partner[0], partner[1], c - rows >= doc, m_ref, acc_ref, False)


def rest_kernel(doc, q_ref, m_in, acc_in, *refs):
    blocks, (o_ref, m_sc, acc_sc) = refs[:6], refs[6:]
    m_sc[...] = m_in[...]
    acc_sc[...] = acc_in[...]
    cell = lax.div(lax.axis_index("ctx"), 2)
    odd = lax.rem(cell, 2)
    size = 2 * q_ref.shape[0]
    for i, other in enumerate((cell - 3 + 2 * odd, cell - 2, cell - 1 - 2 * odd)):
        a, b = blocks[2 * i:2 * i + 2]

        @pl.when((other >= 0) & (other * size >= doc[0]))
        def _(a=a, b=b):
            k = jnp.concatenate([a[0], b[0]], axis=0)
            v = jnp.concatenate([a[1], b[1]], axis=0)
            visit(q_ref, k, v, None, m_sc, acc_sc, False)

    for g in range(GROUP):
        acc = acc_sc[g]
        o_ref[:, g * HD:(g + 1) * HD] = (acc[:, :HD] / acc[:, HD:]).astype(BF16)


def project_kernel(info, *refs):
    left, (w_own, w_mine, w_other, o_ref, a_sc) = refs[:NX], refs[NX:]
    depth = w_mine.shape[1]
    core, part = info[1], info[2]

    @pl.when(pl.program_id(0) == 0)
    def _():
        for d, a in enumerate(left):
            for j, half in enumerate((core, 1 - core) if d else (0, 1)):
                cols = pl.ds(pl.multiple_of(half * depth, depth), depth)
                a_sc[:, (2 * d + j) * depth:(2 * d + j + 1) * depth] = a[:, part, :, cols].reshape(-1, depth)

    total = jnp.dot(a_sc[:, :2 * depth], w_own[...], preferred_element_type=F32)
    for d in range(1, NX):
        for j, w in enumerate((w_mine, w_other)):
            cols = slice((2 * d + j) * depth, (2 * d + j + 1) * depth)
            total = total + jnp.dot(a_sc[:, cols], w[d - 1], preferred_element_type=F32)
    o_ref[...] = total.reshape(o_ref.shape).astype(o_ref.dtype)


def project(info, attended, weight, w_mine, w_other, dtype):
    rows = attended[0].shape[2]
    width = w_mine.shape[2]
    steps = 4
    step = width // steps
    mine = pl.BlockSpec((NX - 1, w_mine.shape[1], step), lambda n, info: (0, 0, n))
    return pl.pallas_call(
        project_kernel,
        out_shape=jax.ShapeDtypeStruct((NX, rows, width), dtype),
        grid_spec=pltpu.PrefetchScalarGridSpec(
            num_scalar_prefetch=1,
            grid=(steps,),
            in_specs=[VMEM] * NX + [
                pl.BlockSpec((weight.shape[0], step), lambda n, info: (0, info[0] * steps + n)),
                mine,
                mine,
            ],
            out_specs=pl.BlockSpec((NX, rows, step), lambda n, info: (0, 0, n)),
            scratch_shapes=[pltpu.VMEM((NX * rows, NX * weight.shape[0]), BF16)],
        ),
        compiler_params=PARAMS,
    )(info, *attended, weight, w_mine, w_other)


def on_device(queries, keys, values, doc_start, out_weight):
    rows = queries.shape[0]
    ctx = lax.axis_index("ctx")
    head = lax.axis_index("head")
    n_ctx = lax.axis_size("ctx")
    core, x, part = ctx % 2, head // 2, head % 2
    swap = [(c, c ^ 1) for c in range(n_ctx)]
    own = jnp.stack([keys, values])

    near = lax.ppermute(own, "ctx", [(c, c + 4) for c in range(n_ctx - 4)])
    jump = [(c, c + (6 if c // 2 % 2 else 2)) for c in range(n_ctx)]
    far = lax.ppermute(own, "ctx", [(c, t) for c, t in jump if t < n_ctx])
    partner = lax.ppermute(own, "ctx", swap)

    width = out_weight.shape[1] // NX
    depth = out_weight.shape[0] // 2
    w_mine = [
        lax.ppermute(w, "head", x_ring(d))
        for d, w in (
            (d, lax.dynamic_slice(out_weight, (core * depth, (x + d) % NX * width), (depth, width)))
            for d in range(1, NX)
        )
    ]

    state = (
        jax.ShapeDtypeStruct((GROUP, rows, HD), F32),
        jax.ShapeDtypeStruct((GROUP, rows, 2 * HD), F32),
    )
    m, acc = pl.pallas_call(
        own_kernel,
        out_shape=state,
        in_specs=[VMEM] * 4,
        out_specs=[VMEM] * 2,
        compiler_params=PARAMS,
    )(queries, doc_start.reshape(-1, HD), own, partner)

    cross = lax.ppermute(near, "ctx", [(c, c ^ 2) for c in range(n_ctx)])
    far_o = lax.ppermute(far, "ctx", swap)
    near_o = lax.ppermute(near, "ctx", swap)
    cross_o = lax.ppermute(cross, "ctx", swap)
    mine = pl.pallas_call(
        rest_kernel,
        out_shape=jax.ShapeDtypeStruct((rows, GROUP * HD), BF16),
        in_specs=[SMEM] + [VMEM] * 9,
        out_specs=VMEM,
        scratch_shapes=[pltpu.VMEM(t.shape, t.dtype) for t in state],
        compiler_params=PARAMS,
    )(doc_start, queries, m, acc, far, far_o, near, near_o, cross, cross_o)

    gathered = [mine] + [lax.ppermute(mine, "head", x_ring(d)) for d in range(1, NX)]
    attended = [a.reshape(NX, 2, rows // NHEAD, -1) for a in gathered]
    w_mine = jnp.stack(lax.optimization_barrier((*w_mine, mine))[:-1])
    w_other = lax.ppermute(w_mine, "ctx", swap)
    info = jnp.stack([x, core, 1 - part, x, core, part]).astype(jnp.int32)
    weights = (out_weight, w_mine, w_other)
    give = project(info[:3], attended, *weights, BF16)
    got = lax.ppermute(give, "head", [(h, h ^ 1) for h in range(NHEAD)])
    keep = project(info[3:], attended, *weights, F32)
    mixed = (keep + got.astype(F32)).astype(BF16)
    groups = [[x * 2 + y for x in range(NX)] for y in range(2)]
    received = lax.all_to_all(mixed, "head", 0, 0, axis_index_groups=groups)
    return received.transpose(1, 0, 2).reshape(rows // NHEAD, NX * width)


def solution(mesh):
    return jax.shard_map(
        on_device,
        mesh=mesh,
        in_specs=(P("ctx", "head"), P("ctx", "head"), P("ctx", "head"), P("ctx"), P("head", None)),
        out_specs=P(("ctx", "head"), None),
        check_vma=False,
    )
```

```python
import jax
import jax.numpy as jnp
from jax import lax
from jax.experimental import pallas as pl
from jax.experimental.pallas import tpu as pltpu
from jax.sharding import PartitionSpec as P


HD = 128
GROUP = 4
NHEAD = 8
NX = 4
NEG = -1.0e30
SCALE2 = HD ** -0.5 * 1.4426950408889634
F32 = jnp.float32
BF16 = jnp.bfloat16


VMEM = pl.BlockSpec(memory_space=pltpu.VMEM)
SMEM = pl.BlockSpec(memory_space=pltpu.SMEM)
PARAMS = pltpu.CompilerParams(vmem_limit_bytes=56 << 20)


def visit(q_ref, k, v, ok, m_sc, acc_sc, first):
    rows = q_ref.shape[0]
    v = jnp.concatenate([v, jnp.ones_like(v)], axis=1)
    scores = [
        lax.dot_general(
            q_ref[:, g * HD:(g + 1) * HD], k, (((1,), (1,)), ((), ())), preferred_element_type=F32
        )
        for g in range(GROUP)
    ]
    for g, s in enumerate(scores):
        if ok is not None:
            s = jnp.where(ok, s, NEG)
        top = jnp.max(s, axis=1, keepdims=True)
        if first:
            m_new = jnp.broadcast_to(top, (rows, HD))
        else:
            m_old = m_sc[g]
            m_new = jnp.maximum(m_old, top)
        base = m_new * SCALE2
        p = jnp.exp2(s * SCALE2 - jnp.tile(base, (1, s.shape[1] // HD)))
        pv = jnp.dot(p.astype(BF16), v, preferred_element_type=F32)
        if first:
            acc_sc[g] = pv
        else:
            factor = jnp.exp2(m_old * SCALE2 - base)
            acc_sc[g] = acc_sc[g] * jnp.tile(factor, (1, 2)) + pv
        m_sc[g] = m_new


def own_kernel(q_ref, doc_ref, own, partner, m_ref, acc_ref):
    rows = q_ref.shape[0]
    ctx = lax.axis_index("ctx")
    r = lax.broadcasted_iota(jnp.int32, (rows, rows), 0)
    c = lax.broadcasted_iota(jnp.int32, (rows, rows), 1)
    groups, lanes = doc_ref.shape
    doc = jnp.concatenate([
        jnp.broadcast_to(doc_ref[i:i + 1], (lanes, lanes)).T for i in range(groups)
    ]) - ctx * rows
    doc = jnp.tile(doc, (1, rows // lanes))
    visit(q_ref, own[0], own[1], (c >= doc) & (c <= r), m_ref, acc_ref, True)

    @pl.when(lax.rem(ctx, 2) == 1)
    def _():
        visit(q_ref, partner[0], partner[1], c - rows >= doc, m_ref, acc_ref, False)


def rest_kernel(doc, q_ref, m_in, acc_in, *refs):
    blocks, refs = refs[:6], refs[6:]
    w_hbm, p_send, p_keep, q_send, q_keep, q_sc, m_sc, acc_sc, w_sc, a_sc, w_sem = refs
    load = pltpu.make_async_copy(w_hbm, w_sc, w_sem)
    load.start()
    q_sc[...] = q_ref[...].reshape(q_sc.shape)
    m_sc[...] = m_in[...].reshape(m_sc.shape)
    acc_sc[...] = acc_in[...].reshape(acc_sc.shape)
    cell = lax.div(lax.axis_index("ctx"), 2)
    odd = lax.rem(cell, 2)
    size = blocks[0].shape[1] * 2
    for i, other in enumerate((cell - 3 + 2 * odd, cell - 2, cell - 1 - 2 * odd)):
        a, b = blocks[2 * i:2 * i + 2]

        @pl.when((other >= 0) & (other * size >= doc[0]))
        def _(a=a, b=b):
            k = jnp.concatenate([a[0], b[0]], axis=0)
            v = jnp.concatenate([a[1], b[1]], axis=0)
            visit(q_sc, k, v, None, m_sc, acc_sc, False)

    for g in range(GROUP):
        acc = acc_sc[g]
        out = (acc[:, :HD] / acc[:, HD:]).astype(BF16)
        a_sc[:, :, g * HD:(g + 1) * HD] = out.reshape(NX, -1, HD)
    load.wait()
    x = lax.div(lax.axis_index("head"), 2)
    near, far = lax.bitwise_xor(x, 1), 3 - x
    half = w_sc.shape[1] // 2
    step = half // 2
    for base, order, send, keep in (
        (0, (near, 3 - near, x, far), p_send, p_keep),
        (half, (far, lax.bitwise_xor(far, 1), x, near), q_send, q_keep),
    ):
        left = jnp.concatenate([a_sc[i] for i in order])
        for n in range(0, half, step):
            part = jnp.dot(left, w_sc[:, base + n:base + n + step], preferred_element_type=F32)
            part = part.astype(BF16).reshape(2, 2, -1, step)
            send[:, :, n:n + step] = part[0]
            keep[:, :, n:n + step] = part[1]


def halve_kernel(p_got, p_keep, q_got, q_keep, p_send, p_next, q_send, q_next):
    for got, keep, send, rest in ((p_got, p_keep, p_send, p_next), (q_got, q_keep, q_send, q_next)):
        rest[...] = (got[0].astype(F32) + keep[0].astype(F32)).astype(BF16)
        send[...] = (got[1].astype(F32) + keep[1].astype(F32)).astype(BF16)


def part_kernel(p_got, p_keep, q_got, q_keep, send, rest):
    part = lax.rem(lax.axis_index("head"), 2)
    rows, half = send.shape[0], p_got.shape[1]
    mine = pl.ds(pl.multiple_of(part * rows, rows), rows)
    give = pl.ds(pl.multiple_of((1 - part) * rows, rows), rows)
    for n, got, keep in ((0, p_got, p_keep), (half, q_got, q_keep)):
        rest[:, n:n + half] = got[mine, :].astype(F32) + keep[mine, :].astype(F32)
        send[:, n:n + half] = (got[give, :].astype(F32) + keep[give, :].astype(F32)).astype(BF16)


def finish_kernel(r0, g0, r1, g1, o_ref):
    rows = r0.shape[0]
    for k, (r, g) in enumerate(((r0, g0), (r1, g1))):
        o_ref[k * rows:(k + 1) * rows, :] = (r[...] + g[...].astype(F32)).astype(BF16)


def on_device(queries, keys, values, doc_start, out_weight):
    rows = queries.shape[0]
    n_ctx = lax.axis_size("ctx")
    swap = [(c, c ^ 1) for c in range(n_ctx)]
    own = jnp.stack([keys, values])

    near = lax.ppermute(own, "ctx", [(c, c + 4) for c in range(n_ctx - 4)])
    jump = [(c, c + (6 if c // 2 % 2 else 2)) for c in range(n_ctx)]
    far = lax.ppermute(own, "ctx", [(c, t) for c, t in jump if t < n_ctx])
    partner = lax.ppermute(own, "ctx", swap)

    state = (
        jax.ShapeDtypeStruct((GROUP, rows, HD), F32),
        jax.ShapeDtypeStruct((GROUP, rows, 2 * HD), F32),
    )
    m, acc = pl.pallas_call(
        own_kernel,
        out_shape=state,
        in_specs=[VMEM] * 4,
        out_specs=[VMEM] * 2,
        compiler_params=PARAMS,
    )(queries, doc_start.reshape(-1, HD), own, partner)

    cross = lax.ppermute(near, "ctx", [(c, c ^ 2) for c in range(n_ctx)])
    far_o = lax.ppermute(far, "ctx", swap)
    near_o = lax.ppermute(near, "ctx", swap)
    cross_o = lax.ppermute(cross, "ctx", swap)
    width = out_weight.shape[1]
    half = width // 2
    block = rows // NHEAD // 2
    shaped = (queries, m, acc)
    shaped = [t.reshape(t.shape[:-2] + (NHEAD, 2, block, t.shape[-1])) for t in shaped]
    to_near = [(h, h ^ 2) for h in range(NHEAD)]
    to_far = [(h, (3 - h // 2) * 2 + h % 2) for h in range(NHEAD)]
    to_part = [(h, h ^ 1) for h in range(NHEAD)]
    vmem = lambda *shapes: [pltpu.VMEM(t, d) for t, d in shapes]
    quad = jax.ShapeDtypeStruct((2, 2 * block, half), BF16)
    pair = jax.ShapeDtypeStruct((2 * block, half), BF16)

    def chunk(k):
        specs = [
            pl.BlockSpec(t.shape[:-3] + (1,) + t.shape[-2:], lambda i, n=t.ndim: (0,) * (n - 3) + (k, 0, 0))
            for t in shaped
        ]
        p_send, p_keep, q_send, q_keep = pl.pallas_call(
            rest_kernel,
            grid=(1,),
            out_shape=[quad] * 4,
            in_specs=[SMEM] + specs + [VMEM] * 6 + [pl.BlockSpec(memory_space=pl.ANY)],
            out_specs=[VMEM] * 4,
            scratch_shapes=vmem(
                ((rows // 2, GROUP * HD), BF16),
                ((GROUP, rows // 2, HD), F32),
                ((GROUP, rows // 2, 2 * HD), F32),
                (out_weight.shape, BF16),
                ((NX, 2 * block, GROUP * HD), BF16),
            ) + [pltpu.SemaphoreType.DMA],
            compiler_params=PARAMS,
        )(doc_start, *shaped, far, far_o, near, near_o, cross, cross_o, out_weight)
        p_got = lax.ppermute(p_send, "head", to_near)
        q_got = lax.ppermute(q_send, "head", to_far)
        p_send, p_keep, q_send, q_keep = pl.pallas_call(
            halve_kernel, out_shape=[pair] * 4, in_specs=[VMEM] * 4, out_specs=[VMEM] * 4
        )(p_got, p_keep, q_got, q_keep)
        p_got = lax.ppermute(p_send, "head", to_far)
        q_got = lax.ppermute(q_send, "head", to_near)
        send, rest = pl.pallas_call(
            part_kernel,
            out_shape=[jax.ShapeDtypeStruct((block, width), t) for t in (BF16, F32)],
            in_specs=[VMEM] * 4,
            out_specs=[VMEM] * 2,
        )(p_got, p_keep, q_got, q_keep)
        return rest, lax.ppermute(send, "head", to_part)

    return pl.pallas_call(
        finish_kernel,
        out_shape=jax.ShapeDtypeStruct((2 * block, width), BF16),
        in_specs=[VMEM] * 4,
        out_specs=VMEM,
    )(*chunk(0), *chunk(1))


def solution(mesh):
    return jax.shard_map(
        on_device,
        mesh=mesh,
        in_specs=(P("ctx", "head"), P("ctx", "head"), P("ctx", "head"), P("ctx"), P("head", None)),
        out_specs=P(("ctx", "head"), None),
        check_vma=False,
    )
```

```python
import jax
import jax.numpy as jnp
from jax import lax
from jax.experimental import pallas as pl
from jax.experimental.pallas import tpu as pltpu
from jax.sharding import PartitionSpec as P


HD = 128
GROUP = 4
NHEAD = 8
NX = 4
NEG = -1.0e30
SCALE2 = HD ** -0.5 * 1.4426950408889634
F32 = jnp.float32
BF16 = jnp.bfloat16


VMEM = pl.BlockSpec(memory_space=pltpu.VMEM)
SMEM = pl.BlockSpec(memory_space=pltpu.SMEM)
PARAMS = pltpu.CompilerParams(vmem_limit_bytes=56 << 20)


def visit(q_ref, k, v, ok, m_sc, acc_sc, first):
    rows = q_ref.shape[0]
    v = jnp.concatenate([v, jnp.ones_like(v)], axis=1)
    scores = [
        lax.dot_general(
            q_ref[:, g * HD:(g + 1) * HD], k, (((1,), (1,)), ((), ())), preferred_element_type=F32
        )
        for g in range(GROUP)
    ]
    for g, s in enumerate(scores):
        if ok is not None:
            s = jnp.where(ok, s, NEG)
        top = jnp.max(s, axis=1, keepdims=True)
        if first:
            m_new = jnp.broadcast_to(top, (rows, HD))
        else:
            m_old = m_sc[g]
            m_new = jnp.maximum(m_old, top)
        base = m_new * SCALE2
        p = jnp.exp2(s * SCALE2 - jnp.tile(base, (1, s.shape[1] // HD)))
        pv = jnp.dot(p.astype(BF16), v, preferred_element_type=F32)
        if first:
            acc_sc[g] = pv
        else:
            factor = jnp.exp2(m_old * SCALE2 - base)
            acc_sc[g] = acc_sc[g] * jnp.tile(factor, (1, 2)) + pv
        m_sc[g] = m_new


def own_kernel(q_ref, doc_ref, own, partner, m_ref, acc_ref):
    rows = q_ref.shape[0]
    ctx = lax.axis_index("ctx")
    r = lax.broadcasted_iota(jnp.int32, (rows, rows), 0)
    c = lax.broadcasted_iota(jnp.int32, (rows, rows), 1)
    groups, lanes = doc_ref.shape
    doc = jnp.concatenate([
        jnp.broadcast_to(doc_ref[i:i + 1], (lanes, lanes)).T for i in range(groups)
    ]) - ctx * rows
    doc = jnp.tile(doc, (1, rows // lanes))
    visit(q_ref, own[0], own[1], (c >= doc) & (c <= r), m_ref, acc_ref, True)

    @pl.when(lax.rem(ctx, 2) == 1)
    def _():
        visit(q_ref, partner[0], partner[1], c - rows >= doc, m_ref, acc_ref, False)


def rest_kernel(doc, q_ref, m_in, acc_in, *refs):
    blocks, refs = refs[:6], refs[6:]
    w_hbm, p_send, p_keep, q_send, q_keep, q_sc, m_sc, acc_sc, w_ref, a_sc, w_sem = refs
    load = pltpu.make_async_copy(w_hbm, w_ref, w_sem)
    load.start()
    q_sc[...] = q_ref[...].reshape(q_sc.shape)
    m_sc[...] = m_in[...].reshape(m_sc.shape)
    acc_sc[...] = acc_in[...].reshape(acc_sc.shape)
    cell = lax.div(lax.axis_index("ctx"), 2)
    odd = lax.rem(cell, 2)
    size = blocks[0].shape[1] * 2
    for i, other in enumerate((cell - 3 + 2 * odd, cell - 2, cell - 1 - 2 * odd)):
        a, b = blocks[2 * i:2 * i + 2]

        @pl.when((other >= 0) & (other * size >= doc[0]))
        def _(a=a, b=b):
            k = jnp.concatenate([a[0], b[0]], axis=0)
            v = jnp.concatenate([a[1], b[1]], axis=0)
            visit(q_sc, k, v, None, m_sc, acc_sc, False)

    for g in range(GROUP):
        acc = acc_sc[g]
        out = (acc[:, :HD] / acc[:, HD:]).astype(BF16)
        a_sc[:, :, g * HD:(g + 1) * HD] = out.reshape(NX, -1, HD)
    load.wait()
    x = lax.div(lax.axis_index("head"), 2)
    near, far = lax.bitwise_xor(x, 1), 3 - x
    half = w_ref.shape[1] // 2
    step = half // 2
    for base, order, send, keep in (
        (0, (near, 3 - near, x, far), p_send, p_keep),
        (half, (far, lax.bitwise_xor(far, 1), x, near), q_send, q_keep),
    ):
        left = jnp.concatenate([a_sc[i] for i in order])
        for n in range(0, half, step):
            part = jnp.dot(left, w_ref[:, base + n:base + n + step], preferred_element_type=F32)
            part = part.astype(BF16).reshape(2, 2, -1, step)
            send[:, :, n:n + step] = part[0]
            keep[:, :, n:n + step] = part[1]


def add(*terms):
    total = terms[0].astype(F32)
    for term in terms[1:]:
        total = total + term.astype(F32)
    return total


def on_device(queries, keys, values, doc_start, out_weight):
    rows = queries.shape[0]
    n_ctx = lax.axis_size("ctx")
    swap = [(c, c ^ 1) for c in range(n_ctx)]
    own = jnp.stack([keys, values])

    near = lax.ppermute(own, "ctx", [(c, c + 4) for c in range(n_ctx - 4)])
    jump = [(c, c + (6 if c // 2 % 2 else 2)) for c in range(n_ctx)]
    far = lax.ppermute(own, "ctx", [(c, t) for c, t in jump if t < n_ctx])
    partner = lax.ppermute(own, "ctx", swap)

    state = (
        jax.ShapeDtypeStruct((GROUP, rows, HD), F32),
        jax.ShapeDtypeStruct((GROUP, rows, 2 * HD), F32),
    )
    m, acc = pl.pallas_call(
        own_kernel,
        out_shape=state,
        in_specs=[VMEM] * 4,
        out_specs=[VMEM] * 2,
        compiler_params=PARAMS,
    )(queries, doc_start.reshape(-1, HD), own, partner)

    cross = lax.ppermute(near, "ctx", [(c, c ^ 2) for c in range(n_ctx)])
    far_o = lax.ppermute(far, "ctx", swap)
    near_o = lax.ppermute(near, "ctx", swap)
    cross_o = lax.ppermute(cross, "ctx", swap)
    part = lax.axis_index("head") % 2
    half = out_weight.shape[1] // 2
    block = rows // NHEAD // 2
    shaped = (queries, m, acc)
    shaped = [t.reshape(t.shape[:-2] + (NHEAD, 2, block, t.shape[-1])) for t in shaped]
    to_near = [(h, h ^ 2) for h in range(NHEAD)]
    to_far = [(h, (3 - h // 2) * 2 + h % 2) for h in range(NHEAD)]
    to_part = [(h, h ^ 1) for h in range(NHEAD)]
    vmem = lambda *shapes: [pltpu.VMEM(t, d) for t, d in shapes]
    quad = jax.ShapeDtypeStruct((2, 2 * block, half), BF16)

    def chunk(k):
        specs = [
            pl.BlockSpec(t.shape[:-3] + (1,) + t.shape[-2:], lambda i, n=t.ndim: (0,) * (n - 3) + (k, 0, 0))
            for t in shaped
        ]
        p_send, p_keep, q_send, q_keep = pl.pallas_call(
            rest_kernel,
            grid=(1,),
            out_shape=[quad] * 4,
            in_specs=[SMEM] + specs + [VMEM] * 6 + [pl.BlockSpec(memory_space=pl.ANY)],
            out_specs=[VMEM] * 4,
            scratch_shapes=vmem(
                ((rows // 2, GROUP * HD), BF16),
                ((GROUP, rows // 2, HD), F32),
                ((GROUP, rows // 2, 2 * HD), F32),
                (out_weight.shape, BF16),
                ((NX, 2 * block, GROUP * HD), BF16),
            ) + [pltpu.SemaphoreType.DMA],
            compiler_params=PARAMS,
        )(doc_start, *shaped, far, far_o, near, near_o, cross, cross_o, out_weight)
        p_got = lax.ppermute(p_send, "head", to_near)
        q_got = lax.ppermute(q_send, "head", to_far)
        p_next = add(p_got[1], p_keep[1]).astype(BF16)
        q_next = add(q_got[1], q_keep[1]).astype(BF16)
        p_last = lax.ppermute(p_next, "head", to_far)
        q_last = lax.ppermute(q_next, "head", to_near)

        def total(y):
            terms = ((p_got, p_keep, p_last), (q_got, q_keep, q_last))
            return jnp.concatenate([
                add(*(lax.dynamic_slice_in_dim(t.reshape(-1, half), y * block, block, 0) for t in side))
                for side in terms
            ], axis=1)

        got = lax.ppermute(total(1 - part).astype(BF16), "head", to_part)
        return (total(part) + got.astype(F32)).astype(BF16)

    return jnp.concatenate([chunk(0), chunk(1)])


def solution(mesh):
    return jax.shard_map(
        on_device,
        mesh=mesh,
        in_specs=(P("ctx", "head"), P("ctx", "head"), P("ctx", "head"), P("ctx"), P("head", None)),
        out_specs=P(("ctx", "head"), None),
        check_vma=False,
    )
```

```python
import jax
import jax.numpy as jnp
from jax import lax
from jax.experimental import pallas as pl
from jax.experimental.pallas import tpu as pltpu
from jax.sharding import PartitionSpec as P


HD = 128
GROUP = 4
NHEAD = 8
W_STEPS = 4
NX = 4
NEG = -1.0e30
SCALE2 = HD ** -0.5 * 1.4426950408889634
F32 = jnp.float32
BF16 = jnp.bfloat16


VMEM = pl.BlockSpec(memory_space=pltpu.VMEM)
SMEM = pl.BlockSpec(memory_space=pltpu.SMEM)
PARAMS = pltpu.CompilerParams(vmem_limit_bytes=56 << 20)


def visit(q_ref, k, v, ok, m_sc, acc_sc, first):
    rows = q_ref.shape[0]
    v = jnp.concatenate([v, jnp.ones_like(v)], axis=1)
    scores = [
        lax.dot_general(
            q_ref[:, g * HD:(g + 1) * HD], k, (((1,), (1,)), ((), ())), preferred_element_type=F32
        )
        for g in range(GROUP)
    ]
    for g, s in enumerate(scores):
        if ok is not None:
            s = jnp.where(ok, s, NEG)
        top = jnp.max(s, axis=1, keepdims=True)
        if first:
            m_new = jnp.broadcast_to(top, (rows, HD))
        else:
            m_old = m_sc[g]
            m_new = jnp.maximum(m_old, top)
        base = m_new * SCALE2
        p = jnp.exp2(s * SCALE2 - jnp.tile(base, (1, s.shape[1] // HD)))
        pv = jnp.dot(p.astype(BF16), v, preferred_element_type=F32)
        if first:
            acc_sc[g] = pv
        else:
            factor = jnp.exp2(m_old * SCALE2 - base)
            acc_sc[g] = acc_sc[g] * jnp.tile(factor, (1, 2)) + pv
        m_sc[g] = m_new


def own_kernel(q_ref, doc_ref, own, partner, m_ref, acc_ref):
    rows = q_ref.shape[0]
    ctx = lax.axis_index("ctx")
    r = lax.broadcasted_iota(jnp.int32, (rows, rows), 0)
    c = lax.broadcasted_iota(jnp.int32, (rows, rows), 1)
    groups, lanes = doc_ref.shape
    doc = jnp.concatenate([
        jnp.broadcast_to(doc_ref[i:i + 1], (lanes, lanes)).T for i in range(groups)
    ]) - ctx * rows
    doc = jnp.tile(doc, (1, rows // lanes))
    visit(q_ref, own[0], own[1], (c >= doc) & (c <= r), m_ref, acc_ref, True)

    @pl.when(lax.rem(ctx, 2) == 1)
    def _():
        visit(q_ref, partner[0], partner[1], c - rows >= doc, m_ref, acc_ref, False)


def rest_kernel(doc, q_ref, m_in, acc_in, *refs):
    blocks, refs = refs[:6], refs[6:]
    w_hbm, p_send, p_keep, q_send, q_keep, q_sc, m_sc, acc_sc, w_ref, a_sc, o_sc, w_sem, o_sem = refs
    step = w_ref.shape[1] // W_STEPS
    loads = [
        pltpu.make_async_copy(
            w_hbm.at[:, n * step:(n + 1) * step], w_ref.at[:, n * step:(n + 1) * step], w_sem.at[n]
        )
        for n in range(W_STEPS)
    ]
    for load in loads:
        load.start()
    q_sc[...] = q_ref[...].reshape(q_sc.shape)
    m_sc[...] = m_in[...].reshape(m_sc.shape)
    acc_sc[...] = acc_in[...].reshape(acc_sc.shape)
    cell = lax.div(lax.axis_index("ctx"), 2)
    odd = lax.rem(cell, 2)
    size = blocks[0].shape[1] * 2
    for i, other in enumerate((cell - 3 + 2 * odd, cell - 2, cell - 1 - 2 * odd)):
        a, b = blocks[2 * i:2 * i + 2]

        @pl.when((other >= 0) & (other * size >= doc[0]))
        def _(a=a, b=b):
            k = jnp.concatenate([a[0], b[0]], axis=0)
            v = jnp.concatenate([a[1], b[1]], axis=0)
            visit(q_sc, k, v, None, m_sc, acc_sc, False)

    for g in range(GROUP):
        acc = acc_sc[g]
        out = (acc[:, :HD] / acc[:, HD:]).astype(BF16)
        a_sc[:, :, g * HD:(g + 1) * HD] = out.reshape(NX, -1, HD)
    x = lax.div(lax.axis_index("head"), 2)
    near, far = lax.bitwise_xor(x, 1), 3 - x
    sides = (
        ((near, 3 - near, x, far), p_send, p_keep),
        ((far, lax.bitwise_xor(far, 1), x, near), q_send, q_keep),
    )
    stores = []
    for i, (order, *outs) in enumerate(sides):
        left = jnp.concatenate([a_sc[j] for j in order])
        for n in range(W_STEPS // 2):
            k = i * (W_STEPS // 2) + n
            loads[k].wait()
            part = jnp.dot(left, w_ref[:, k * step:(k + 1) * step], preferred_element_type=F32)
            o_sc[k] = part.astype(BF16).reshape(o_sc.shape[1:])
            for j, out in enumerate(outs):
                stores.append(pltpu.make_async_copy(
                    o_sc.at[k, j], out.at[:, :, n * step:(n + 1) * step], o_sem.at[2 * k + j]
                ))
                stores[-1].start()
    for store in stores:
        store.wait()


def add(*terms):
    total = terms[0].astype(F32)
    for term in terms[1:]:
        total = total + term.astype(F32)
    return total


def on_device(queries, keys, values, doc_start, out_weight):
    rows = queries.shape[0]
    n_ctx = lax.axis_size("ctx")
    swap = [(c, c ^ 1) for c in range(n_ctx)]
    own = jnp.stack([keys, values])

    near = lax.ppermute(own, "ctx", [(c, c + 4) for c in range(n_ctx - 4)])
    jump = [(c, c + (6 if c // 2 % 2 else 2)) for c in range(n_ctx)]
    far = lax.ppermute(own, "ctx", [(c, t) for c, t in jump if t < n_ctx])
    partner = lax.ppermute(own, "ctx", swap)

    state = (
        jax.ShapeDtypeStruct((GROUP, rows, HD), F32),
        jax.ShapeDtypeStruct((GROUP, rows, 2 * HD), F32),
    )
    m, acc = pl.pallas_call(
        own_kernel,
        out_shape=state,
        in_specs=[VMEM] * 4,
        out_specs=[VMEM] * 2,
        compiler_params=PARAMS,
    )(queries, doc_start.reshape(-1, HD), own, partner)

    cross = lax.ppermute(near, "ctx", [(c, c ^ 2) for c in range(n_ctx)])
    far_o = lax.ppermute(far, "ctx", swap)
    near_o = lax.ppermute(near, "ctx", swap)
    cross_o = lax.ppermute(cross, "ctx", swap)
    part = lax.axis_index("head") % 2
    half = out_weight.shape[1] // 2
    block = rows // NHEAD // 2
    shaped = (queries, m, acc)
    shaped = [t.reshape(t.shape[:-2] + (NHEAD, 2, block, t.shape[-1])) for t in shaped]
    to_near = [(h, h ^ 2) for h in range(NHEAD)]
    to_far = [(h, (3 - h // 2) * 2 + h % 2) for h in range(NHEAD)]
    to_part = [(h, h ^ 1) for h in range(NHEAD)]
    vmem = lambda *shapes: [pltpu.VMEM(t, d) for t, d in shapes]
    quad = jax.ShapeDtypeStruct((2, 2 * block, half), BF16)

    def chunk(k):
        specs = [
            pl.BlockSpec(t.shape[:-3] + (1,) + t.shape[-2:], lambda i, n=t.ndim: (0,) * (n - 3) + (k, 0, 0))
            for t in shaped
        ]
        p_send, p_keep, q_send, q_keep = pl.pallas_call(
            rest_kernel,
            grid=(1,),
            out_shape=[quad] * 4,
            in_specs=[SMEM] + specs + [VMEM] * 6 + [pl.BlockSpec(memory_space=pl.ANY)],
            out_specs=[pl.BlockSpec(memory_space=pl.ANY)] * 4,
            scratch_shapes=vmem(
                ((rows // 2, GROUP * HD), BF16),
                ((GROUP, rows // 2, HD), F32),
                ((GROUP, rows // 2, 2 * HD), F32),
                (out_weight.shape, BF16),
                ((NX, 2 * block, GROUP * HD), BF16),
                ((W_STEPS, 2, 2, 2 * block, 2 * half // W_STEPS), BF16),
            ) + [pltpu.SemaphoreType.DMA((W_STEPS,)), pltpu.SemaphoreType.DMA((2 * W_STEPS,))],
            compiler_params=PARAMS,
        )(doc_start, *shaped, far, far_o, near, near_o, cross, cross_o, out_weight)
        p_got = lax.ppermute(p_send, "head", to_near)
        q_got = lax.ppermute(q_send, "head", to_far)
        p_next = add(p_got[1], p_keep[1]).astype(BF16)
        q_next = add(q_got[1], q_keep[1]).astype(BF16)
        p_last = lax.ppermute(p_next, "head", to_far)
        q_last = lax.ppermute(q_next, "head", to_near)

        def total(y):
            terms = ((p_got, p_keep, p_last), (q_got, q_keep, q_last))
            return jnp.concatenate([
                add(*(lax.dynamic_slice_in_dim(t.reshape(-1, half), y * block, block, 0) for t in side))
                for side in terms
            ], axis=1)

        got = lax.ppermute(total(1 - part).astype(BF16), "head", to_part)
        return (total(part) + got.astype(F32)).astype(BF16)

    return jnp.concatenate([chunk(0), chunk(1)])


def solution(mesh):
    return jax.shard_map(
        on_device,
        mesh=mesh,
        in_specs=(P("ctx", "head"), P("ctx", "head"), P("ctx", "head"), P("ctx"), P("head", None)),
        out_specs=P(("ctx", "head"), None),
        check_vma=False,
    )
```

```python
import jax
import jax.numpy as jnp
from jax import lax
from jax.experimental import pallas as pl
from jax.experimental.pallas import tpu as pltpu
from jax.sharding import PartitionSpec as P


HD = 128
GROUP = 4
NHEAD = 8
W_STEPS = 4
NX = 4
NEG = -1.0e30
SCALE2 = HD ** -0.5 * 1.4426950408889634
F32 = jnp.float32
BF16 = jnp.bfloat16


VMEM = pl.BlockSpec(memory_space=pltpu.VMEM)
SMEM = pl.BlockSpec(memory_space=pltpu.SMEM)
PARAMS = pltpu.CompilerParams(vmem_limit_bytes=56 << 20)


def visit(q_ref, k, v, ok, m_sc, acc_sc, first):
    rows = q_ref.shape[0]
    v = jnp.concatenate([v, jnp.ones_like(v)], axis=1)
    scores = [
        lax.dot_general(
            q_ref[:, g * HD:(g + 1) * HD], k, (((1,), (1,)), ((), ())), preferred_element_type=F32
        )
        for g in range(GROUP)
    ]
    for g, s in enumerate(scores):
        if ok is not None:
            s = jnp.where(ok, s, NEG)
        top = jnp.max(s, axis=1, keepdims=True)
        if first:
            m_new = jnp.broadcast_to(top, (rows, HD))
        else:
            m_old = m_sc[g]
            m_new = jnp.maximum(m_old, top)
        base = m_new * SCALE2
        p = jnp.exp2(s * SCALE2 - jnp.tile(base, (1, s.shape[1] // HD)))
        pv = jnp.dot(p.astype(BF16), v, preferred_element_type=F32)
        if first:
            acc_sc[g] = pv
        else:
            factor = jnp.exp2(m_old * SCALE2 - base)
            acc_sc[g] = acc_sc[g] * jnp.tile(factor, (1, 2)) + pv
        m_sc[g] = m_new


def own_docs(doc_ref, rows):
    groups, lanes = doc_ref.shape
    doc = jnp.concatenate([
        jnp.broadcast_to(doc_ref[i:i + 1], (lanes, lanes)).T for i in range(groups)
    ]) - lax.axis_index("ctx") * rows
    return jnp.tile(doc, (1, rows // lanes))


def own_kernel(q_ref, doc_ref, own, m_ref, acc_ref):
    rows = q_ref.shape[0]
    r = lax.broadcasted_iota(jnp.int32, (rows, rows), 0)
    c = lax.broadcasted_iota(jnp.int32, (rows, rows), 1)
    doc = own_docs(doc_ref, rows)
    visit(q_ref, own[0], own[1], (c >= doc) & (c <= r), m_ref, acc_ref, True)


def middle_kernel(first, q_ref, doc_ref, m_in, acc_in, partner, near, near_o, m_ref, acc_ref):
    rows = q_ref.shape[0]
    m_ref[...] = m_in[...]
    acc_ref[...] = acc_in[...]
    ctx = lax.axis_index("ctx")

    @pl.when(lax.rem(ctx, 2) == 1)
    def _():
        c = lax.broadcasted_iota(jnp.int32, (rows, rows), 1)
        seen = c - rows >= own_docs(doc_ref, rows)
        visit(q_ref, partner[0], partner[1], seen, m_ref, acc_ref, False)

    other = lax.div(ctx, 2) - 2

    @pl.when((other >= 0) & (other * 2 * rows >= first[0]))
    def _():
        k = jnp.concatenate([near[0], near_o[0]], axis=0)
        v = jnp.concatenate([near[1], near_o[1]], axis=0)
        visit(q_ref, k, v, None, m_ref, acc_ref, False)


def rest_kernel(doc, q_ref, m_in, acc_in, *refs):
    blocks, refs = refs[:4], refs[4:]
    w_hbm, p_send, p_keep, q_send, q_keep, q_sc, m_sc, acc_sc, w_ref, a_sc, o_sc, w_sem, o_sem = refs
    step = w_ref.shape[1] // W_STEPS
    loads = [
        pltpu.make_async_copy(
            w_hbm.at[:, n * step:(n + 1) * step], w_ref.at[:, n * step:(n + 1) * step], w_sem.at[n]
        )
        for n in range(W_STEPS)
    ]
    for load in loads:
        load.start()
    q_sc[...] = q_ref[...].reshape(q_sc.shape)
    m_sc[...] = m_in[...].reshape(m_sc.shape)
    acc_sc[...] = acc_in[...].reshape(acc_sc.shape)
    cell = lax.div(lax.axis_index("ctx"), 2)
    odd = lax.rem(cell, 2)
    size = blocks[0].shape[1] * 2
    for i, other in enumerate((cell - 3 + 2 * odd, cell - 1 - 2 * odd)):
        a, b = blocks[2 * i:2 * i + 2]

        @pl.when((other >= 0) & (other * size >= doc[0]))
        def _(a=a, b=b):
            k = jnp.concatenate([a[0], b[0]], axis=0)
            v = jnp.concatenate([a[1], b[1]], axis=0)
            visit(q_sc, k, v, None, m_sc, acc_sc, False)

    for g in range(GROUP):
        acc = acc_sc[g]
        out = (acc[:, :HD] / acc[:, HD:]).astype(BF16)
        a_sc[:, :, g * HD:(g + 1) * HD] = out.reshape(NX, -1, HD)
    x = lax.div(lax.axis_index("head"), 2)
    near, far = lax.bitwise_xor(x, 1), 3 - x
    sides = (
        ((near, 3 - near, x, far), p_send, p_keep),
        ((far, lax.bitwise_xor(far, 1), x, near), q_send, q_keep),
    )
    stores = []
    for i, (order, *outs) in enumerate(sides):
        left = jnp.concatenate([a_sc[j] for j in order])
        for n in range(W_STEPS // 2):
            k = i * (W_STEPS // 2) + n
            loads[k].wait()
            part = jnp.dot(left, w_ref[:, k * step:(k + 1) * step], preferred_element_type=F32)
            o_sc[k] = part.astype(BF16).reshape(o_sc.shape[1:])
            for j, out in enumerate(outs):
                stores.append(pltpu.make_async_copy(
                    o_sc.at[k, j], out.at[:, :, n * step:(n + 1) * step], o_sem.at[2 * k + j]
                ))
                stores[-1].start()
    for store in stores:
        store.wait()


def add(*terms):
    total = terms[0].astype(F32)
    for term in terms[1:]:
        total = total + term.astype(F32)
    return total


def on_device(queries, keys, values, doc_start, out_weight):
    rows = queries.shape[0]
    ctx = lax.axis_index("ctx")
    n_ctx = lax.axis_size("ctx")
    swap = [(c, c ^ 1) for c in range(n_ctx)]
    own = jnp.stack([keys, values])

    near = lax.ppermute(own, "ctx", [(c, c + 4) for c in range(n_ctx - 4)])
    passed = jnp.where(ctx // 2 % 2 == 1, near, own)
    far = lax.ppermute(passed, "ctx", [(c, c + 2) for c in range(n_ctx - 2)])
    partner = lax.ppermute(own, "ctx", swap)

    state = (
        jax.ShapeDtypeStruct((GROUP, rows, HD), F32),
        jax.ShapeDtypeStruct((GROUP, rows, 2 * HD), F32),
    )
    docs = doc_start.reshape(-1, HD)
    m, acc = pl.pallas_call(
        own_kernel,
        out_shape=state,
        in_specs=[VMEM] * 3,
        out_specs=[VMEM] * 2,
        compiler_params=PARAMS,
    )(queries, docs, own)

    cross = lax.ppermute(near, "ctx", [(c, c ^ 2) for c in range(n_ctx)])
    far_o = lax.ppermute(far, "ctx", swap)
    near_o = lax.ppermute(near, "ctx", swap)
    cross_o = lax.ppermute(cross, "ctx", swap)
    m, acc = pl.pallas_call(
        middle_kernel,
        out_shape=state,
        in_specs=[SMEM] + [VMEM] * 7,
        out_specs=[VMEM] * 2,
        compiler_params=PARAMS,
    )(doc_start, queries, docs, m, acc, partner, near, near_o)
    part = lax.axis_index("head") % 2
    half = out_weight.shape[1] // 2
    block = rows // NHEAD // 2
    shaped = (queries, m, acc)
    shaped = [t.reshape(t.shape[:-2] + (NHEAD, 2, block, t.shape[-1])) for t in shaped]
    to_near = [(h, h ^ 2) for h in range(NHEAD)]
    to_far = [(h, (3 - h // 2) * 2 + h % 2) for h in range(NHEAD)]
    to_part = [(h, h ^ 1) for h in range(NHEAD)]
    vmem = lambda *shapes: [pltpu.VMEM(t, d) for t, d in shapes]
    quad = jax.ShapeDtypeStruct((2, 2 * block, half), BF16)

    def chunk(k):
        specs = [
            pl.BlockSpec(t.shape[:-3] + (1,) + t.shape[-2:], lambda i, n=t.ndim: (0,) * (n - 3) + (k, 0, 0))
            for t in shaped
        ]
        p_send, p_keep, q_send, q_keep = pl.pallas_call(
            rest_kernel,
            grid=(1,),
            out_shape=[quad] * 4,
            in_specs=[SMEM] + specs + [VMEM] * 4 + [pl.BlockSpec(memory_space=pl.ANY)],
            out_specs=[pl.BlockSpec(memory_space=pl.ANY)] * 4,
            scratch_shapes=vmem(
                ((rows // 2, GROUP * HD), BF16),
                ((GROUP, rows // 2, HD), F32),
                ((GROUP, rows // 2, 2 * HD), F32),
                (out_weight.shape, BF16),
                ((NX, 2 * block, GROUP * HD), BF16),
                ((W_STEPS, 2, 2, 2 * block, 2 * half // W_STEPS), BF16),
            ) + [pltpu.SemaphoreType.DMA((W_STEPS,)), pltpu.SemaphoreType.DMA((2 * W_STEPS,))],
            compiler_params=PARAMS,
        )(doc_start, *shaped, far, far_o, cross, cross_o, out_weight)
        p_got = lax.ppermute(p_send, "head", to_near)
        q_got = lax.ppermute(q_send, "head", to_far)
        p_next = add(p_got[1], p_keep[1]).astype(BF16)
        q_next = add(q_got[1], q_keep[1]).astype(BF16)
        p_last = lax.ppermute(p_next, "head", to_far)
        q_last = lax.ppermute(q_next, "head", to_near)

        def total(y):
            terms = ((p_got, p_keep, p_last), (q_got, q_keep, q_last))
            return jnp.concatenate([
                add(*(lax.dynamic_slice_in_dim(t.reshape(-1, half), y * block, block, 0) for t in side))
                for side in terms
            ], axis=1)

        got = lax.ppermute(total(1 - part).astype(BF16), "head", to_part)
        return (total(part) + got.astype(F32)).astype(BF16)

    mixed = jnp.zeros((2 * block, 2 * half), BF16)
    for k in range(2):
        mixed = lax.dynamic_update_slice(mixed, chunk(k), (k * block, 0))
    return mixed


def solution(mesh):
    return jax.shard_map(
        on_device,
        mesh=mesh,
        in_specs=(P("ctx", "head"), P("ctx", "head"), P("ctx", "head"), P("ctx"), P("head", None)),
        out_specs=P(("ctx", "head"), None),
        check_vma=False,
    )
```

```python
import jax
import jax.numpy as jnp
from jax import lax
from jax.experimental import pallas as pl
from jax.experimental.pallas import tpu as pltpu
from jax.sharding import PartitionSpec as P


HD = 128
GROUP = 4
NHEAD = 8
W_STEPS = 4
NX = 4
NEG = -1.0e30
SCALE2 = HD ** -0.5 * 1.4426950408889634
F32 = jnp.float32
BF16 = jnp.bfloat16


VMEM = pl.BlockSpec(memory_space=pltpu.VMEM)
SMEM = pl.BlockSpec(memory_space=pltpu.SMEM)
PARAMS = pltpu.CompilerParams(vmem_limit_bytes=56 << 20)


def visit(q_ref, k, v, ok, m_sc, acc_sc, first):
    rows = q_ref.shape[0]
    v = jnp.concatenate([v, jnp.ones_like(v)], axis=1)
    scores = [
        lax.dot_general(
            q_ref[:, g * HD:(g + 1) * HD], k, (((1,), (1,)), ((), ())), preferred_element_type=F32
        )
        for g in range(GROUP)
    ]
    for g, s in enumerate(scores):
        if ok is not None:
            s = jnp.where(ok, s, NEG)
        top = jnp.max(s, axis=1, keepdims=True)
        if first:
            m_new = jnp.broadcast_to(top, (rows, HD))
        else:
            m_old = m_sc[g]
            m_new = jnp.maximum(m_old, top)
        base = m_new * SCALE2
        p = jnp.exp2(s * SCALE2 - jnp.tile(base, (1, s.shape[1] // HD)))
        pv = jnp.dot(p.astype(BF16), v, preferred_element_type=F32)
        if first:
            acc_sc[g] = pv
        else:
            factor = jnp.exp2(m_old * SCALE2 - base)
            acc_sc[g] = acc_sc[g] * jnp.tile(factor, (1, 2)) + pv
        m_sc[g] = m_new


def own_kernel(q_ref, doc_ref, own, partner, m_ref, acc_ref):
    rows = q_ref.shape[0]
    ctx = lax.axis_index("ctx")
    r = lax.broadcasted_iota(jnp.int32, (rows, rows), 0)
    c = lax.broadcasted_iota(jnp.int32, (rows, rows), 1)
    groups, lanes = doc_ref.shape
    doc = jnp.concatenate([
        jnp.broadcast_to(doc_ref[i:i + 1], (lanes, lanes)).T for i in range(groups)
    ]) - ctx * rows
    doc = jnp.tile(doc, (1, rows // lanes))
    visit(q_ref, own[0], own[1], (c >= doc) & (c <= r), m_ref, acc_ref, True)

    @pl.when(lax.rem(ctx, 2) == 1)
    def _():
        visit(q_ref, partner[0], partner[1], c - rows >= doc, m_ref, acc_ref, False)


def rest_kernel(doc, q_ref, m_in, acc_in, *refs):
    blocks, refs = refs[:6], refs[6:]
    w_hbm, p_send, p_keep, q_send, q_keep, q_sc, m_sc, acc_sc, w_ref, a_sc, o_sc, w_sem, o_sem = refs
    step = w_ref.shape[1] // W_STEPS
    loads = [
        pltpu.make_async_copy(
            w_hbm.at[:, n * step:(n + 1) * step], w_ref.at[:, n * step:(n + 1) * step], w_sem.at[n]
        )
        for n in range(W_STEPS)
    ]
    for load in loads:
        load.start()
    q_sc[...] = q_ref[...].reshape(q_sc.shape)
    m_sc[...] = m_in[...].reshape(m_sc.shape)
    acc_sc[...] = acc_in[...].reshape(acc_sc.shape)
    cell = lax.div(lax.axis_index("ctx"), 2)
    odd = lax.rem(cell, 2)
    size = blocks[0].shape[1] * 2
    for i, other in enumerate((cell - 3 + 2 * odd, cell - 2, cell - 1 - 2 * odd)):
        a, b = blocks[2 * i:2 * i + 2]

        @pl.when((other >= 0) & (other * size >= doc[0]))
        def _(a=a, b=b):
            k = jnp.concatenate([a[0], b[0]], axis=0)
            v = jnp.concatenate([a[1], b[1]], axis=0)
            visit(q_sc, k, v, None, m_sc, acc_sc, False)

    for g in range(GROUP):
        acc = acc_sc[g]
        out = (acc[:, :HD] / acc[:, HD:]).astype(BF16)
        a_sc[:, :, g * HD:(g + 1) * HD] = out.reshape(NX, -1, HD)
    x = lax.div(lax.axis_index("head"), 2)
    near, far = lax.bitwise_xor(x, 1), 3 - x
    sides = (
        ((near, 3 - near, x, far), p_send, p_keep),
        ((far, lax.bitwise_xor(far, 1), x, near), q_send, q_keep),
    )
    stores = []
    for i, (order, *outs) in enumerate(sides):
        left = jnp.concatenate([a_sc[j] for j in order])
        for n in range(W_STEPS // 2):
            k = i * (W_STEPS // 2) + n
            loads[k].wait()
            part = jnp.dot(left, w_ref[:, k * step:(k + 1) * step], preferred_element_type=F32)
            o_sc[k] = part.astype(BF16).reshape(o_sc.shape[1:])
            for j, out in enumerate(outs):
                stores.append(pltpu.make_async_copy(
                    o_sc.at[k, j], out.at[:, :, n * step:(n + 1) * step], o_sem.at[2 * k + j]
                ))
                stores[-1].start()
    for store in stores:
        store.wait()


def add(*terms):
    total = terms[0].astype(F32)
    for term in terms[1:]:
        total = total + term.astype(F32)
    return total


def on_device(queries, keys, values, doc_start, out_weight):
    rows = queries.shape[0]
    ctx = lax.axis_index("ctx")
    n_ctx = lax.axis_size("ctx")
    swap = [(c, c ^ 1) for c in range(n_ctx)]
    own = jnp.stack([keys, values])

    near = lax.ppermute(own, "ctx", [(c, c + 4) for c in range(n_ctx - 4)])
    passed = jnp.where(ctx // 2 % 2 == 1, near, own)
    far = lax.ppermute(passed, "ctx", [(c, c + 2) for c in range(n_ctx - 2)])
    partner = lax.ppermute(own, "ctx", swap)

    state = (
        jax.ShapeDtypeStruct((GROUP, rows, HD), F32),
        jax.ShapeDtypeStruct((GROUP, rows, 2 * HD), F32),
    )
    m, acc = pl.pallas_call(
        own_kernel,
        out_shape=state,
        in_specs=[VMEM] * 4,
        out_specs=[VMEM] * 2,
        compiler_params=PARAMS,
    )(queries, doc_start.reshape(-1, HD), own, partner)

    cross = lax.ppermute(near, "ctx", [(c, c ^ 2) for c in range(n_ctx)])
    far_o = lax.ppermute(far, "ctx", swap)
    near_o = lax.ppermute(near, "ctx", swap)
    cross_o = lax.ppermute(cross, "ctx", swap)
    part = lax.axis_index("head") % 2
    half = out_weight.shape[1] // 2
    block = rows // NHEAD // 2
    shaped = (queries, m, acc)
    shaped = [t.reshape(t.shape[:-2] + (NHEAD, 2, block, t.shape[-1])) for t in shaped]
    to_near = [(h, h ^ 2) for h in range(NHEAD)]
    to_far = [(h, (3 - h // 2) * 2 + h % 2) for h in range(NHEAD)]
    to_part = [(h, h ^ 1) for h in range(NHEAD)]
    vmem = lambda *shapes: [pltpu.VMEM(t, d) for t, d in shapes]
    quad = jax.ShapeDtypeStruct((2, 2 * block, half), BF16)

    def chunk(k):
        specs = [
            pl.BlockSpec(t.shape[:-3] + (1,) + t.shape[-2:], lambda i, n=t.ndim: (0,) * (n - 3) + (k, 0, 0))
            for t in shaped
        ]
        p_send, p_keep, q_send, q_keep = pl.pallas_call(
            rest_kernel,
            grid=(1,),
            out_shape=[quad] * 4,
            in_specs=[SMEM] + specs + [VMEM] * 6 + [pl.BlockSpec(memory_space=pl.ANY)],
            out_specs=[pl.BlockSpec(memory_space=pl.ANY)] * 4,
            scratch_shapes=vmem(
                ((rows // 2, GROUP * HD), BF16),
                ((GROUP, rows // 2, HD), F32),
                ((GROUP, rows // 2, 2 * HD), F32),
                (out_weight.shape, BF16),
                ((NX, 2 * block, GROUP * HD), BF16),
                ((W_STEPS, 2, 2, 2 * block, 2 * half // W_STEPS), BF16),
            ) + [pltpu.SemaphoreType.DMA((W_STEPS,)), pltpu.SemaphoreType.DMA((2 * W_STEPS,))],
            compiler_params=PARAMS,
        )(doc_start, *shaped, far, far_o, near, near_o, cross, cross_o, out_weight)
        p_got = lax.ppermute(p_send, "head", to_near)
        q_got = lax.ppermute(q_send, "head", to_far)
        p_next = add(p_got[1], p_keep[1]).astype(BF16)
        q_next = add(q_got[1], q_keep[1]).astype(BF16)
        p_last = lax.ppermute(p_next, "head", to_far)
        q_last = lax.ppermute(q_next, "head", to_near)

        def total(y):
            terms = ((p_got, p_keep, p_last), (q_got, q_keep, q_last))
            return jnp.concatenate([
                add(*(lax.dynamic_slice_in_dim(t.reshape(-1, half), y * block, block, 0) for t in side))
                for side in terms
            ], axis=1)

        got = lax.ppermute(total(1 - part).astype(BF16), "head", to_part)
        return (total(part) + got.astype(F32)).astype(BF16)

    return jnp.concatenate([chunk(0), chunk(1)])


def solution(mesh):
    return jax.shard_map(
        on_device,
        mesh=mesh,
        in_specs=(P("ctx", "head"), P("ctx", "head"), P("ctx", "head"), P("ctx"), P("head", None)),
        out_specs=P(("ctx", "head"), None),
        check_vma=False,
    )
```
